32 devices in a mesh: section: 4 (over y, x), peer: 8 (over z, core).
Axes of the slice: x: 2, y: 2, z: 4, core: 2. Of those that a mesh axis runs over, the one named last changes fastest.
Arguments:
- inbox: bfloat16 [4, 8, 128, 5120], P('section', 'peer'), may hold values from -6 to 6
- routes: int32 [4, 8, 8], replicated, may hold values from 0 to 4, as said below
- adapter_in: bfloat16 [4, 2, 16, 5120], P('section'), may hold values from -0.078125 to 0.078125
- adapter_out: bfloat16 [4, 2, 16, 5120], P('section'), may hold values from -1.5 to 1.5
- returned: bfloat16 [4, 8, 160, 5120], P('section', 'peer'), may hold values from -6 to 6
Outputs:
- handed: bfloat16 [4, 8, 160, 5120], P('section', 'peer')
- mean_in: float32 [4, 2, 16, 5120], P('section', None, None, 'peer')
- mean_out: float32 [4, 2, 16, 5120], P('section', None, None, 'peer')
The draws below stay inside these ranges and needn't reach their ends.
Inputs may be any that keep to these rules, and one draw needn't show every extreme that they name: routes[s, p, q] is how many micro-batches peer p of section s sends to peer q of the next section; every row sums to 16; every column sums to at most 20, and in every section some column reaches 20; some entry of every section reaches 4.
All inputs are finite; a program needn't handle non-finite values.
Results may differ from the reference program's by a relative error of at most 0.015.
Values may be sent and summed in bfloat16 or wider, within the bound.
No kernel may reach another device: no remote copies, remote signals or barrier semaphores. Data moves between devices by JAX's collectives and lax.ppermute only.
A program may use at most 64 MiB of HBM per device.

```python
import jax
import jax.numpy as jnp
from jax import lax

D = 5120
RANK = 16
LAYERS = 2
MB = 8
MICRO = 16
TOK_DEV = 128
PEERS = 8
SECTIONS = 4
PAIR = 4
CAP = 20


def one_table(key):
    hot_count = max(1, PEERS // 8)
    rest_total = PEERS * MICRO - hot_count * CAP
    others = PEERS - hot_count
    base_load = rest_total // others
    extra_load = rest_total % others
    ranks = jnp.arange(PEERS, dtype=jnp.int32)
    demand_by_rank = jnp.where(ranks < hot_count, CAP, base_load + (ranks - hot_count < extra_load).astype(jnp.int32))
    order = jax.random.permutation(jax.random.fold_in(key, 1), PEERS)
    demand = jnp.zeros((PEERS,), jnp.int32).at[order].set(demand_by_rank.astype(jnp.int32))
    noise_key = jax.random.fold_in(key, 2)

    def row_step(row, carry):
        table, remaining = carry

        def unit_step(unit, inner):
            counts, left = inner
            noise = jax.random.permutation(jax.random.fold_in(noise_key, row * MICRO + unit), PEERS).astype(jnp.int32)
            eligible = (counts < PAIR) & (left > 0)
            score = jnp.where(eligible, left * 4096 + noise, -1)
            chosen = lax.top_k(score, 1)[1][0]
            hit = (jnp.arange(PEERS, dtype=jnp.int32) == chosen).astype(jnp.int32)
            return (counts + hit, left - hit)
        counts, remaining = lax.fori_loop(0, MICRO, unit_step, (jnp.zeros((PEERS,), jnp.int32), remaining))
        table = lax.dynamic_update_slice(table, counts[None, :], (row, 0))
        return (table, remaining)
    table, remaining = lax.fori_loop(0, PEERS, row_step, (jnp.zeros((PEERS, PEERS), jnp.int32), demand))
    return table


def draw_routes(key, part):
    keys = jax.random.split(key, SECTIONS)
    return jax.vmap(one_table)(keys)


def level_of(rng, shape, shards, smallest, high):
    loudness = 1.0
    for dim, parts in shards:
        draws = jax.random.uniform(jax.random.fold_in(jax.random.fold_in(rng, 6), dim), (parts,), jnp.float32, smallest / len(shards), high / len(shards))
        loudness = loudness * jnp.repeat(jnp.exp(draws), shape[dim] // parts).reshape((-1,) + (1,) * (len(shape) - 1 - dim))
    return loudness


def normal_values(own_key, extent, scale, bound, cuts=(), held_as=jnp.bfloat16):
    array = jax.random.normal(own_key, extent, jnp.float32) * scale
    if len(cuts) > 0:
        array = level_of(own_key, extent, cuts, -0.22, 0.18) * array
    return jnp.clip(array, min=-bound, max=bound).astype(held_as)


def setup_inputs(seed: int = 0) -> dict:
    key_list = jax.random.split(jax.random.key(seed), 6)
    return {
        "inbox": normal_values(key_list[0], (SECTIONS, PEERS, TOK_DEV, D), 1.0, 6.0, ((0, 4), (1, 8))),
        "routes": draw_routes(jax.random.fold_in(key_list[5], 71), 0),
        "adapter_in": normal_values(key_list[2], (SECTIONS, LAYERS, RANK, D), D ** -0.5, 0.078125, ((0, 4),)),
        "adapter_out": normal_values(key_list[3], (SECTIONS, LAYERS, RANK, D), RANK ** -0.5, 1.5, ((0, 4),)),
        "returned": normal_values(key_list[4], (SECTIONS, PEERS, CAP * MB, D), 1.0, 6.0, ((0, 4), (1, 8))),
    }


epsilon = 1e-06

def inverse_rms(hidden):
    return lax.rsqrt(lax.optimization_barrier(jnp.mean(hidden * hidden, axis=-1, keepdims=True)) + epsilon)

def contract_last(left, right):
    return lax.dot_general(left, right, (((1,), (1,)), ((), ())), preferred_element_type=jnp.float32)

def contract_first(left, right):
    return lax.dot_general(left, right, (((0,), (0,)), ((), ())), preferred_element_type=jnp.float32)

def section_forward(inputs, weight_in, weight_out):
    hidden = inputs.astype(jnp.float32)
    for layer in range(weight_in.shape[0]):
        normed = (hidden * inverse_rms(hidden)).astype(jnp.bfloat16)
        lowered = contract_last(normed, weight_in[layer]).astype(jnp.bfloat16)
        hidden = hidden + jnp.dot(lowered, weight_out[layer], preferred_element_type=jnp.float32)
    return hidden.astype(jnp.bfloat16)

def section_backward(inputs, weight_in, weight_out, incoming):
    hidden = inputs.astype(jnp.float32)
    saved = []
    for layer in range(weight_in.shape[0]):
        saved.append(hidden)
        normed = (hidden * inverse_rms(hidden)).astype(jnp.bfloat16)
        lowered = contract_last(normed, weight_in[layer]).astype(jnp.bfloat16)
        hidden = hidden + jnp.dot(lowered, weight_out[layer], preferred_element_type=jnp.float32)
    grad = incoming.astype(jnp.float32)
    grads_in = []
    grads_out = []
    for layer in reversed(range(weight_in.shape[0])):
        hidden = saved[layer]
        scale = inverse_rms(hidden)
        plain = hidden * scale
        normed = plain.astype(jnp.bfloat16)
        lowered = contract_last(normed, weight_in[layer]).astype(jnp.bfloat16)
        grad_bf = grad.astype(jnp.bfloat16)
        grads_out.append(contract_first(lowered, grad_bf))
        back_low = contract_last(grad_bf, weight_out[layer]).astype(jnp.bfloat16)
        grads_in.append(contract_first(back_low, normed))
        if layer > 0:
            spread = jnp.dot(back_low, weight_in[layer], preferred_element_type=jnp.float32)
            grad = grad + scale * (spread - plain * lax.optimization_barrier(jnp.mean(spread * plain, axis=-1, keepdims=True)))
    return (jnp.stack(grads_in[::-1]), jnp.stack(grads_out[::-1]))

def slot_sources(counts):
    sent_end = jnp.cumsum(counts, axis=1)
    sent_start = sent_end - counts
    slot_start = jnp.cumsum(counts, axis=0) - counts
    slot_end = slot_start + counts
    positions = jnp.arange(CAP, dtype=jnp.int32)
    owner = lax.optimization_barrier(jnp.sum((slot_end.T[:, :, None] <= positions[None, None, :]).astype(jnp.int32), axis=1))
    valid = positions[None, :] < lax.optimization_barrier(jnp.sum(counts, axis=0))[:, None]
    owner = jnp.minimum(owner, PEERS - 1).astype(jnp.int32)
    offset = positions[None, :] - jnp.take_along_axis(slot_start.T, owner, axis=1)
    micro_index = jnp.take_along_axis(sent_start.T, owner, axis=1) + offset
    micro_index = jnp.where(valid, micro_index, 0)
    return ((owner * MICRO + micro_index).astype(jnp.int32), valid)

def send_targets(counts):
    sent_end = jnp.cumsum(counts, axis=1)
    sent_start = sent_end - counts
    slot_start = jnp.cumsum(counts, axis=0) - counts
    micro = jnp.arange(MICRO, dtype=jnp.int32)
    target = lax.optimization_barrier(jnp.sum((sent_end[:, None, :] <= micro[None, :, None]).astype(jnp.int32), axis=2)).astype(jnp.int32)
    offset = micro[None, :] - jnp.take_along_axis(sent_start, target, axis=1)
    slot = jnp.take_along_axis(slot_start, target, axis=1) + offset
    return (target, slot.astype(jnp.int32))

def reference(inbox, routes, adapter_in, adapter_out, returned):
    width = inbox.shape[-1]

    def forward_one(section_args):
        inputs, weight_in, weight_out = section_args
        return jax.vmap(section_forward, in_axes=(0, None, None))(inputs, weight_in, weight_out)
    outgoing = lax.map(forward_one, (inbox, adapter_in, adapter_out))

    def deliver(section_args):
        produced, counts = section_args
        sources, valid = slot_sources(counts)
        blocks = produced.reshape(PEERS * MICRO, MB, width)
        picked = blocks[sources]
        picked = jnp.where(valid[:, :, None, None], picked, jnp.zeros((), picked.dtype))
        return picked.reshape(PEERS, CAP * MB, width)
    handed = lax.map(deliver, (jnp.roll(outgoing, 1, axis=0), jnp.roll(routes, 1, axis=0)))

    def backward_one(section_args):
        inputs, weight_in, weight_out, slots_next, counts = section_args
        target, slot = send_targets(counts)
        arriving = slots_next.reshape(PEERS, CAP, MB, width)[target, slot]
        arriving = arriving.reshape(PEERS, MICRO * MB, width)
        terms_in, terms_out = jax.vmap(section_backward, in_axes=(0, None, None, 0))(inputs, weight_in, weight_out, arriving)
        return (lax.optimization_barrier(jnp.sum(terms_in, axis=0)) / PEERS, lax.optimization_barrier(jnp.sum(terms_out, axis=0)) / PEERS)
    mean_in, mean_out = lax.map(backward_one, (inbox, adapter_in, adapter_out, jnp.roll(returned, -1, axis=0), routes))
    return (handed, mean_in, mean_out)
```

```python
import functools

import jax
import jax.numpy as jnp
from jax import lax
from jax.experimental import pallas as pl
from jax.experimental.pallas import tpu as pltpu
from jax.sharding import PartitionSpec as P

MB = 8
EPSILON = 1e-06


def partner(peer, offset):
    return peer ^ offset


def column_block(width):
    for block in (1024, 512, 256, 128):
        if width % block == 0:
            return block
    return width


def hop_pairs(sections, peers, by, offset):
    return [
        (s * peers + p, ((s + by) % sections) * peers + partner(p, offset))
        for s in range(sections)
        for p in range(peers)
    ]


def send_kernel(peers, slots, micro, routes, inbox, w_in, w_out, *refs):
    outs, w_half = refs[:peers], refs[peers]
    stage, w_stage, in_sem, out_sem, w_sem, starts = refs[peers + 1 :]
    section = lax.axis_index("section")
    peer = lax.axis_index("peer")
    total = jnp.int32(0)
    for q in range(peers):
        starts[q] = total
        total = total + routes[section, peer, q]

    def load(d, t):
        j = jnp.minimum(starts[partner(peer, d)] + t, micro - 1)
        return pltpu.make_async_copy(inbox.at[j], stage.at[d, t], in_sem.at[d, t])

    def store(d):
        return pltpu.make_async_copy(stage.at[d], outs[d], out_sem.at[d])

    even = lax.rem(peer, 2) == 0
    w_load_in = pltpu.make_async_copy(w_in, w_stage, w_sem.at[0])
    w_load_out = pltpu.make_async_copy(w_out, w_stage, w_sem.at[0])
    w_store = pltpu.make_async_copy(w_stage, w_half, w_sem.at[1])
    for d in range(peers):
        for t in range(slots):
            load(d, t).start()

    @pl.when(even)
    def _():
        w_load_in.start()

    @pl.when(jnp.logical_not(even))
    def _():
        w_load_out.start()

    for d in range(peers):
        for t in range(slots):
            load(d, t).wait()
        store(d).start()
    w_load_in.wait()
    w_store.start()
    for d in range(peers):
        store(d).wait()
    w_store.wait()


def contract_last(left, right):
    return lax.dot_general(
        left, right, (((1,), (1,)), ((), ())), preferred_element_type=jnp.float32
    )


def contract_first(left, right):
    return lax.dot_general(
        left, right, (((0,), (0,)), ((), ())), preferred_element_type=jnp.float32
    )


def expand(left, right):
    return jnp.dot(left, right, preferred_element_type=jnp.float32)


def step_kernel(
    peers, sections, slots, capacity, group, rank, routes, returned, w_half, w_other, *refs
):
    arrived = refs[:peers]
    handed, keep, give = refs[peers : peers + 3]
    (x_buf, n0, n1, g1, h1, lows, backs, w, terms, x_sem, w_sem, starts) = refs[peers + 3 :]
    width = x_buf.shape[-1]
    block = column_block(width)
    blocks = [slice(c * block, (c + 1) * block) for c in range(width // block)]
    section = lax.axis_index("section")
    peer = lax.axis_index("peer")
    earlier = lax.rem(section + sections - 1, sections)
    parity = lax.rem(peer, 2)
    w_copies = [
        pltpu.make_async_copy(w_half, w.at[parity], w_sem.at[0]),
        pltpu.make_async_copy(w_other, w.at[1 - parity], w_sem.at[1]),
    ]
    for copy in w_copies:
        copy.start()
    total = jnp.int32(0)
    for p in range(peers):
        starts[p] = total
        total = total + routes[earlier, p, peer]

    def each_slot(action):
        for d in range(peers):
            p = partner(peer, d)
            for t in range(slots):

                @pl.when(t < routes[earlier, p, peer])
                def _():
                    k = starts[p] + t
                    action(pltpu.make_async_copy(arrived[d].at[t], x_buf.at[k], x_sem.at[d, t]))

    each_slot(lambda copy: copy.start())

    @pl.loop(0, capacity)
    def _(k):
        @pl.when(k >= total)
        def _():
            x_buf[k] = jnp.zeros((MB, width), x_buf.dtype)

    each_slot(lambda copy: copy.wait())
    for copy in w_copies:
        copy.wait()
    rows = group * MB

    def lane_sum(value):
        part = value[:, :128]
        for c in range(1, value.shape[1] // 128):
            part = part + value[:, c * 128 : (c + 1) * 128]
        return part

    def mean_of(part):
        return jnp.sum(part, axis=-1, keepdims=True) / width

    @pl.loop(0, capacity // group)
    def _(i):
        k = pl.ds(i * group, group)
        r = pl.ds(pl.multiple_of(i * rows, rows), rows)

        def x_at(c):
            return x_buf[k, :, c].astype(jnp.float32).reshape(rows, block)

        def g_at(c):
            return returned[k, :, c].astype(jnp.float32).reshape(rows, block)

        part = jnp.zeros((rows, 128), jnp.float32)
        back1 = jnp.zeros((rows, rank), jnp.float32)
        for c in blocks:
            x = x_at(c)
            part = part + lane_sum(x * x)
            back1 = back1 + contract_last(g_at(c).astype(jnp.bfloat16), w[1, 1, :, c])
        scale0 = lax.rsqrt(mean_of(part) + EPSILON)
        back1 = back1.astype(jnp.bfloat16)
        low0 = jnp.zeros((rows, rank), jnp.float32)
        for c in blocks:
            normed = (x_at(c) * scale0).astype(jnp.bfloat16)
            n0[r, c] = normed
            low0 = low0 + contract_last(normed, w[0, 0, :, c])
        low0 = low0.astype(jnp.bfloat16)
        part = jnp.zeros((rows, 128), jnp.float32)
        for c in blocks:
            hidden = x_at(c) + expand(low0, w[1, 0, :, c])
            h1[:, c] = hidden
            part = part + lane_sum(hidden * hidden)
        scale1 = lax.rsqrt(mean_of(part) + EPSILON)
        low1 = jnp.zeros((rows, rank), jnp.float32)
        for c in blocks:
            normed = (h1[:, c] * scale1).astype(jnp.bfloat16)
            n1[r, c] = normed
            low1 = low1 + contract_last(normed, w[0, 1, :, c])
        mean = jnp.sum(back1.astype(jnp.float32) * low1, axis=-1, keepdims=True) / width
        pull = scale1 * scale1 * mean
        low1 = low1.astype(jnp.bfloat16)
        back0 = jnp.zeros((rows, rank), jnp.float32)
        for c in blocks:
            hidden = h1[:, c]
            out = hidden + expand(low1, w[1, 1, :, c])
            handed[k, :, c] = out.reshape(group, MB, block).astype(handed.dtype)
            grad = g_at(c) + (scale1 * expand(back1, w[0, 1, :, c]) - hidden * pull)
            grad = grad.astype(jnp.bfloat16)
            g1[r, c] = grad
            back0 = back0 + contract_last(grad, w[1, 0, :, c])
        lows[0, r] = low0
        lows[1, r] = low1
        backs[0, r] = back0.astype(jnp.bfloat16)
        backs[1, r] = back1

    for c in blocks:
        g = returned[:, :, c].astype(jnp.float32).reshape(capacity * MB, block).astype(jnp.bfloat16)
        terms[0 * rank : 1 * rank, c] = contract_first(backs[0], n0[:, c])
        terms[1 * rank : 2 * rank, c] = contract_first(backs[1], n1[:, c])
        terms[2 * rank : 3 * rank, c] = contract_first(lows[0], g1[:, c])
        terms[3 * rank : 4 * rank, c] = contract_first(lows[1], g)
    part_width = width // peers
    if part_width % 128 == 0:
        for z in range(peers // 2):
            mine = pl.multiple_of((2 * z + parity) * part_width, 128)
            theirs = pl.multiple_of((2 * z + 1 - parity) * part_width, 128)
            keep[z] = terms[:, pl.ds(mine, part_width)]
            give[z] = terms[:, pl.ds(theirs, part_width)].astype(give.dtype)
    else:
        for z in range(peers // 2):
            first = terms[:, 2 * z * part_width : (2 * z + 1) * part_width]
            second = terms[:, (2 * z + 1) * part_width : (2 * z + 2) * part_width]
            keep[z] = jnp.where(parity == 0, first, second)
            give[z] = jnp.where(parity == 0, second, first).astype(give.dtype)


def pair_kernel(groups, keep, got, *outs):
    half = lax.div(lax.axis_index("peer"), 2)
    for e in range(groups):
        z = partner(half, e)
        outs[e][...] = (keep[z] + got[z].astype(jnp.float32)).astype(outs[e].dtype)


def shards(inbox, routes, adapter_in, adapter_out, returned):
    peers = lax.axis_size("peer")
    sections = lax.axis_size("section")
    tokens, width = inbox.shape[2:]
    layers, rank = adapter_in.shape[1:3]
    micro = tokens // MB
    slots = max(1, 2 * micro // peers)
    capacity = returned.shape[2] // MB
    group = 4 if capacity % 4 == 0 else 1
    rows = capacity * MB
    vmem = pl.BlockSpec(memory_space=pltpu.VMEM)
    smem = pl.BlockSpec(memory_space=pltpu.SMEM)
    hbm = pl.BlockSpec(memory_space=pl.ANY)
    bf16 = jnp.bfloat16
    axes = ("section", "peer")

    sent = pl.pallas_call(
        functools.partial(send_kernel, peers, slots, micro),
        out_shape=[jax.ShapeDtypeStruct((slots, MB, width), bf16)] * peers
        + [jax.ShapeDtypeStruct((layers, rank, width), bf16)],
        in_specs=[smem, hbm, hbm, hbm],
        out_specs=[hbm] * (peers + 1),
        scratch_shapes=[
            pltpu.VMEM((peers, slots, MB, width), bf16),
            pltpu.VMEM((layers, rank, width), bf16),
            pltpu.SemaphoreType.DMA((peers, slots)),
            pltpu.SemaphoreType.DMA((peers,)),
            pltpu.SemaphoreType.DMA((2,)),
            pltpu.SMEM((peers,), jnp.int32),
        ],
        cost_estimate=pl.CostEstimate(flops=0, bytes_accessed=4 * tokens * width * 2, transcendentals=0),
    )(routes, inbox[0, 0].reshape(micro, MB, width), adapter_in[0], adapter_out[0])
    w_half = lax.ppermute(sent[peers], axes, hop_pairs(sections, peers, 1, 0))
    order = sorted(range(peers), key=lambda d: -d)
    arrived = [None] * peers
    for d in order:
        arrived[d] = lax.ppermute(sent[d], axes, hop_pairs(sections, peers, 1, d))
    w_other = lax.ppermute(w_half, "peer", [(p, p ^ 1) for p in range(peers)])

    part_width = width // peers
    handed, keep, give = pl.pallas_call(
        functools.partial(step_kernel, peers, sections, slots, capacity, group, rank),
        out_shape=[
            jax.ShapeDtypeStruct((capacity, MB, width), bf16),
            jax.ShapeDtypeStruct((peers // 2, 2 * layers * rank, part_width), jnp.float32),
            jax.ShapeDtypeStruct((peers // 2, 2 * layers * rank, part_width), bf16),
        ],
        in_specs=[smem, vmem, hbm, hbm] + [hbm] * peers,
        out_specs=[vmem, vmem, vmem],
        scratch_shapes=[
            pltpu.VMEM((capacity, MB, width), bf16),
            pltpu.VMEM((rows, width), bf16),
            pltpu.VMEM((rows, width), bf16),
            pltpu.VMEM((rows, width), bf16),
            pltpu.VMEM((group * MB, width), jnp.float32),
            pltpu.VMEM((layers, rows, rank), bf16),
            pltpu.VMEM((layers, rows, rank), bf16),
            pltpu.VMEM((2, layers, rank, width), bf16),
            pltpu.VMEM((2 * layers * rank, width), jnp.float32),
            pltpu.SemaphoreType.DMA((peers, slots)),
            pltpu.SemaphoreType.DMA((2,)),
            pltpu.SMEM((peers,), jnp.int32),
        ],
        cost_estimate=pl.CostEstimate(
            flops=22 * rows * width * rank, bytes_accessed=8 * tokens * width * 2, transcendentals=0
        ),
    )(routes, returned[0, 0].reshape(capacity, MB, width), w_half, w_other, *arrived)

    got = lax.ppermute(give, "peer", [(p, p ^ 1) for p in range(peers)])
    summed = pl.pallas_call(
        functools.partial(pair_kernel, peers // 2),
        out_shape=[jax.ShapeDtypeStruct((2 * layers * rank, part_width), bf16)] * (peers // 2),
        in_specs=[vmem, vmem],
        out_specs=[vmem] * (peers // 2),
    )(keep, got)
    pieces = [
        lax.ppermute(piece, axes, hop_pairs(sections, peers, -1, 2 * e))
        for e, piece in enumerate(summed)
    ]
    mean = functools.reduce(jnp.add, [piece.astype(jnp.float32) for piece in pieces]) / peers
    mean = mean.reshape(2, 1, layers, rank, part_width)
    return (handed.reshape(1, 1, rows, width), mean[0], mean[1])


def solution(mesh):
    return jax.shard_map(
        shards,
        mesh=mesh,
        in_specs=(
            P("section", "peer", None, None),
            P(),
            P("section", None, None, None),
            P("section", None, None, None),
            P("section", "peer", None, None),
        ),
        out_specs=(
            P("section", "peer", None, None),
            P("section", None, None, "peer"),
            P("section", None, None, "peer"),
        ),
        check_vma=False,
    )
```

```python
import functools

import jax
import jax.numpy as jnp
from jax import lax
from jax.experimental import pallas as pl
from jax.experimental.pallas import tpu as pltpu
from jax.sharding import PartitionSpec as P

MB = 8
EPSILON = 1e-06
GROUP = 4
VMEM_LIMIT = 20 * 2**20


BF16 = jnp.bfloat16
HBM = pl.BlockSpec(memory_space=pl.ANY)
SMEM = pl.BlockSpec(memory_space=pltpu.SMEM)


class Plan:
    def __init__(self, sections, peers, micro, capacity):
        self.sections, self.peers, self.micro, self.capacity = sections, peers, micro, capacity
        self.chips = peers // 2
        pair = max(1, 2 * micro // peers)
        self.full = 2 * pair
        self.relay = pair % 2 == 0 and pair * self.chips == micro
        self.base = pair if self.relay else self.full
        half = self.base // 2
        self.sets = [(half, self.base), (0, half)] if self.relay else [(0, self.base)]


def hop_pairs(plan, by, offset):
    return [
        (s * plan.peers + p, ((s + by) % plan.sections) * plan.peers + (p ^ offset))
        for s in range(plan.sections)
        for p in range(plan.peers)
    ]


def to_sibling(plan, array):
    return lax.ppermute(array, "peer", [(p, p ^ 1) for p in range(plan.peers)])


def prefix(values):
    starts, total = [], jnp.int32(0)
    for value in values:
        starts.append(total)
        total = total + value
    return starts, total


class Row:
    def __init__(self, plan, routes, section, sender):
        self.base = plan.base
        self.counts = [
            routes[section, sender, 2 * c] + routes[section, sender, 2 * c + 1]
            for c in range(plan.chips)
        ]
        self.over = [jnp.maximum(n - plan.base, 0) for n in self.counts]
        self.free = [jnp.maximum(plan.base - n, 0) for n in self.counts]
        self.over_start, self.over_total = prefix(self.over)
        self.free_start, _ = prefix(self.free)

    def shared(self, relay, chip):
        first = jnp.maximum(self.free_start[relay], self.over_start[chip])
        last = jnp.minimum(
            self.free_start[relay] + self.free[relay], self.over_start[chip] + self.over[chip]
        )
        return first, jnp.maximum(last - first, 0)


def send_kernel(plan, positions, carry_weights, routes, inbox, *refs):
    chips, base = plan.chips, plan.base
    weights = refs[:2] if carry_weights else ()
    refs = refs[len(weights) :]
    outs = [refs[i * chips : (i + 1) * chips] for i in range(len(positions))]
    refs = refs[len(positions) * chips :]
    if carry_weights:
        w_half, refs = refs[0], refs[1:]
        w_stage, w_sem, refs = refs[0], refs[1], refs[2:]
    stage, in_sem, out_sem = refs[:3]
    section = lax.axis_index("section")
    peer = lax.axis_index("peer")
    chip = lax.div(peer, 2)
    row = Row(plan, routes, section, peer)
    start, _ = prefix(row.counts)
    source = refs[3]
    for c in range(chips):
        for u in range(plan.full):
            own = start[c] + u
            if u >= base or not plan.relay:
                source[c, u] = jnp.minimum(own, plan.micro - 1)
                continue
            index = row.free_start[c] + (base - 1 - u)
            other = jnp.int32(0)
            for b in range(chips):
                o = index - row.over_start[b]
                inside = jnp.logical_and(o >= 0, o < row.over[b])
                other = jnp.where(inside, start[b] + base + o, other)
            source[c, u] = jnp.where(u < row.counts[c], own, other)

    order = [(i, e) for i in range(len(positions)) for e in reversed(range(chips))]

    def load(e, u):
        return pltpu.make_async_copy(
            inbox.at[source[chip ^ e, u]], stage.at[e, u - first], in_sem.at[e, u - first]
        )

    first = min(a for a, _ in positions)
    if carry_weights:
        even = lax.rem(peer, 2) == 0
        w_load = [pltpu.make_async_copy(weight, w_stage, w_sem.at[0]) for weight in weights]
        w_store = pltpu.make_async_copy(w_stage, w_half, w_sem.at[1])
    for i, e in order:
        for u in range(*positions[i]):
            load(e, u).start()
    if carry_weights:
        pl.when(even)(lambda: w_load[0].start())
        pl.when(jnp.logical_not(even))(lambda: w_load[1].start())

    def store(i, e):
        a, b = positions[i]
        return pltpu.make_async_copy(
            stage.at[e, a - first : b - first], outs[i][e], out_sem.at[i, e]
        )

    for i, e in order:
        for u in range(*positions[i]):
            load(e, u).wait()
        store(i, e).start()
    if carry_weights:
        w_load[0].wait()
        w_store.start()
    for i, e in order:
        store(i, e).wait()
    if carry_weights:
        w_store.wait()


def run_send(plan, positions, routes, blocks, weights=()):
    width = blocks.shape[-1]
    chips = plan.chips
    span = max(b for _, b in positions) - min(a for a, _ in positions)
    out_shape = [
        jax.ShapeDtypeStruct((b - a, MB, width), BF16) for a, b in positions for _ in range(chips)
    ]
    scratch = []
    if weights:
        out_shape.append(jax.ShapeDtypeStruct(weights[0].shape, BF16))
        scratch = [pltpu.VMEM(weights[0].shape, BF16), pltpu.SemaphoreType.DMA((2,))]
    return pl.pallas_call(
        functools.partial(send_kernel, plan, positions, bool(weights)),
        out_shape=out_shape,
        in_specs=[SMEM] + [HBM] * (1 + len(weights)),
        out_specs=[HBM] * len(out_shape),
        scratch_shapes=scratch
        + [
            pltpu.VMEM((chips, span, MB, width), BF16),
            pltpu.SemaphoreType.DMA((chips, span)),
            pltpu.SemaphoreType.DMA((len(positions), chips)),
            pltpu.SMEM((chips, plan.full), jnp.int32),
        ],
        compiler_params=pltpu.CompilerParams(vmem_limit_bytes=VMEM_LIMIT),
    )(routes, blocks, *weights)


def table_kernel(plan, routes, *maps):
    chips, base = plan.chips, plan.base
    section = lax.axis_index("section")
    peer = lax.axis_index("peer")
    chip = lax.div(peer, 2)
    core = lax.rem(peer, 2)
    earlier = lax.rem(section + plan.sections - 1, plan.sections)
    starts = maps[-1]
    total = jnp.int32(0)
    for p in range(plan.peers):
        starts[p] = total
        total = total + routes[earlier, p, peer]

    def slot(sender, position, usable):
        zero = routes[earlier, sender, 2 * chip]
        one = routes[earlier, sender, 2 * chip + 1]
        to_one = position >= zero
        mine = jnp.logical_and(to_one == (core == 1), position < zero + one)
        t = position - jnp.where(to_one, zero, 0)
        return jnp.where(jnp.logical_and(mine, usable), starts[sender] + t, -1)

    set_maps = maps[: len(plan.sets)]
    for (a, b), out in zip(plan.sets, set_maps):
        for lane in range(2):
            for e in range(chips):
                sender = 2 * (chip ^ e) + (core ^ lane)
                for u in range(a, b):
                    out[(lane * chips + e) * (b - a) + u - a] = slot(sender, jnp.int32(u), True)
    if not plan.relay:
        return
    extra_map, picks, relay_map, fits, rows = maps[len(plan.sets) : -1]
    span = plan.full - base
    for lane in range(2):
        for e in range(chips):
            sender = 2 * (chip ^ e) + (core ^ lane)
            for u in range(base, plan.full):
                extra_map[(lane * chips + e) * span + u - base] = slot(sender, jnp.int32(u), True)

    def all_fit(s, fit):
        shared = [[jnp.int32(0)] * chips for _ in range(chips)]
        for sender in range(plan.peers):
            row = Row(plan, routes, s, sender)
            for r in range(chips):
                used = jnp.minimum(row.free_start[r] + row.free[r], row.over_total)
                fit = jnp.logical_and(fit, used - row.free_start[r] <= base - base // 2)
                for c in range(chips):
                    if r != c:
                        shared[r][c] = shared[r][c] + row.shared(r, c)[1]
        for r in range(chips):
            for c in range(chips):
                fit = jnp.logical_and(fit, shared[r][c] <= 2)
        return fit

    fit = lax.fori_loop(0, plan.sections, all_fit, jnp.bool_(True))
    fits[0] = fit.astype(jnp.int32)
    for sender in range(plan.peers):
        row = Row(plan, routes, earlier, sender)
        for c in range(chips):
            rows[0, sender, c] = row.over_start[c]
            rows[1, sender, c] = row.over[c]
            rows[2, sender, c] = row.free_start[c]
            rows[3, sender, c] = row.free[c]

    def find(relay, target, number):
        seen = jnp.int32(0)
        found = (jnp.int32(-1), jnp.int32(0), jnp.int32(0))
        for sender in range(plan.peers):
            first = jnp.maximum(rows[2, sender, relay], rows[0, sender, target])
            last = jnp.minimum(
                rows[2, sender, relay] + rows[3, sender, relay],
                rows[0, sender, target] + rows[1, sender, target],
            )
            count = jnp.maximum(last - first, 0)
            here = jnp.logical_and(number >= seen, number < seen + count)
            index = first + number - seen
            found = (
                jnp.where(here, sender, found[0]),
                jnp.where(here, index - rows[0, sender, target], found[1]),
                jnp.where(here, base - 1 - (index - rows[2, sender, relay]), found[2]),
            )
            seen = seen + count
        return found

    a, b = plan.sets[0]
    for f in range(1, chips):
        sender, _, u = find(chip, chip ^ f, core)
        lane = lax.rem(sender, 2) ^ core
        e = lax.div(sender, 2) ^ chip
        code = (lane * chips + e) * (b - a) + u - a
        picks[f] = jnp.where(jnp.logical_and(sender >= 0, u >= a), code, 0)
        for lane in range(2):
            sender, item, _ = find(chip ^ f, chip, core ^ lane)
            usable = jnp.logical_and(sender >= 0, fit)
            place = slot(jnp.maximum(sender, 0), base + item, usable)
            relay_map[lane * (chips - 1) + f - 1] = place


def run_tables(plan, routes):
    chips = plan.chips
    sizes = [2 * chips * (b - a) for a, b in plan.sets]
    scratch = []
    if plan.relay:
        sizes += [2 * chips * (plan.full - plan.base), chips, 2 * (chips - 1), 1]
        scratch = [pltpu.SMEM((4, plan.peers, chips), jnp.int32)]
    return pl.pallas_call(
        functools.partial(table_kernel, plan),
        out_shape=[jax.ShapeDtypeStruct((n,), jnp.int32) for n in sizes],
        in_specs=[SMEM],
        out_specs=[SMEM] * len(sizes),
        scratch_shapes=scratch + [pltpu.SMEM((plan.peers,), jnp.int32)],
    )(routes)


def pick_kernel(plan, picks, *refs):
    chips = plan.chips
    sources = refs[: 2 * chips]
    outs = refs[2 * chips : 3 * chips - 1]
    stage, in_sem, out_sem = refs[3 * chips - 1 :]
    slots = sources[0].shape[0]

    def each(f, action):
        for i, source in enumerate(sources):
            for u in range(slots):

                @pl.when(picks[f] == i * slots + u)
                def _():
                    action(pltpu.make_async_copy(source.at[u], stage.at[f], in_sem.at[f]))

    def store(f):
        return pltpu.make_async_copy(stage.at[f], outs[f - 1].at[0], out_sem.at[f])

    for f in range(1, chips):
        each(f, lambda copy: copy.start())
    for f in range(1, chips):
        pltpu.make_async_copy(sources[0].at[0], stage.at[f], in_sem.at[f]).wait()
        store(f).start()
    for f in range(1, chips):
        store(f).wait()


def run_picks(plan, picks, sources):
    width = sources[0].shape[-1]
    return pl.pallas_call(
        functools.partial(pick_kernel, plan),
        out_shape=[jax.ShapeDtypeStruct((1, MB, width), BF16)] * (plan.chips - 1),
        in_specs=[SMEM] + [HBM] * len(sources),
        out_specs=[HBM] * (plan.chips - 1),
        scratch_shapes=[
            pltpu.VMEM((plan.chips, MB, width), BF16),
            pltpu.SemaphoreType.DMA((plan.chips,)),
            pltpu.SemaphoreType.DMA((plan.chips,)),
        ],
        compiler_params=pltpu.CompilerParams(vmem_limit_bytes=VMEM_LIMIT),
    )(picks, *sources)


def contract_last(left, right):
    return lax.dot_general(
        left, right, (((1,), (1,)), ((), ())), preferred_element_type=jnp.float32
    )


def expand(left, right):
    return jnp.dot(left, right, preferred_element_type=jnp.float32)


def column_block(width):
    for block in (512, 256, 128):
        if width % block == 0:
            return block
    return width


def step_kernel(plan, rank, counts, first, last, routes, *refs):
    maps, refs = refs[: len(counts)], refs[len(counts) :]
    sources, refs = refs[: sum(counts)], refs[sum(counts) :]
    returned, w_half, w_other = refs[:3]
    refs = refs[3:]
    if not first:
        terms_in, refs = refs[1], refs[2:]
    handed, refs = refs[0], refs[1:]
    if last:
        keep, give, refs = refs[0], refs[1], refs[2:]
    else:
        terms_out, refs = refs[0], refs[1:]
    (x_buf, g_buf, out_buf, n0, n1, g1, h1, w, terms) = refs[:9]
    (x_sem, g_sem, out_sem, w_sem, t_sem, zero_sem, places) = refs[9:]
    capacity = plan.capacity
    width = x_buf.shape[-1]
    block = column_block(width)
    blocks = [slice(c * block, (c + 1) * block) for c in range(width // block)]
    section = lax.axis_index("section")
    peer = lax.axis_index("peer")
    parity = lax.rem(peer, 2)
    candidates = []
    i = 0
    for count, table in zip(counts, maps):
        for j in range(count):
            slots = sources[i + j].shape[0]
            for u in range(slots):
                candidates.append((sources[i + j].at[u], table, j * slots + u))
        i += count

    def fetch(source, k, n):
        return [
            pltpu.make_async_copy(source, x_buf.at[n], x_sem.at[n]),
            pltpu.make_async_copy(returned.at[k], g_buf.at[n], g_sem.at[n]),
        ]

    n = jnp.int32(0)
    for source, table, index in candidates:
        k = table[index]

        @pl.when(k >= 0)
        def _():
            places[n] = k
            for copy in fetch(source, k, n):
                copy.start()

        n = n + (k >= 0).astype(jnp.int32)
    w_copies = [
        pltpu.make_async_copy(w_half, w.at[parity], w_sem.at[0]),
        pltpu.make_async_copy(w_other, w.at[1 - parity], w_sem.at[1]),
    ]
    for copy in w_copies:
        copy.start()
    if first:
        earlier = lax.rem(section + plan.sections - 1, plan.sections)
        total = jnp.int32(0)
        for p in range(plan.peers):
            total = total + routes[earlier, p, peer]
        h1[0:MB, :] = jnp.zeros((MB, width), jnp.float32)
        out_buf[capacity] = h1[0:MB, :].astype(BF16)

        @pl.loop(total, capacity)
        def _(k):
            pltpu.make_async_copy(out_buf.at[capacity], handed.at[k], zero_sem.at[k]).start()

        terms[...] = jnp.zeros(terms.shape, jnp.float32)
    else:
        copy = pltpu.make_async_copy(terms_in, terms, t_sem)
        copy.start()
    groups = lax.div(n + GROUP - 1, GROUP)

    @pl.loop(n, groups * GROUP)
    def _(i):
        x_buf[i] = jnp.zeros((MB, width), BF16)
        g_buf[i] = jnp.zeros((MB, width), BF16)

    for copy in w_copies:
        copy.wait()
    if not first:
        pltpu.make_async_copy(terms_in, terms, t_sem).wait()
    rows = GROUP * MB

    def lane_sum(value):
        part = value[:, :128]
        for c in range(1, value.shape[1] // 128):
            part = part + value[:, c * 128 : (c + 1) * 128]
        return part

    def mean_of(part):
        return jnp.sum(part, axis=-1, keepdims=True) / width

    @pl.loop(0, groups)
    def _(i):
        k = pl.ds(i * GROUP, GROUP)

        @pl.loop(i * GROUP, jnp.minimum(n, (i + 1) * GROUP))
        def _(j):
            for copy in fetch(candidates[0][0], 0, j):
                copy.wait()

        def x_at(c):
            return x_buf[k, :, c].astype(jnp.float32).reshape(rows, block)

        def g_at(c):
            return g_buf[k, :, c].astype(jnp.float32).reshape(rows, block)

        part = jnp.zeros((rows, 128), jnp.float32)
        back1 = jnp.zeros((rows, rank), jnp.float32)
        for c in blocks:
            x = x_at(c)
            part = part + lane_sum(x * x)
            back1 = back1 + contract_last(g_at(c).astype(BF16), w[1, 1, :, c])
        scale0 = lax.rsqrt(mean_of(part) + EPSILON)
        low0 = jnp.zeros((rows, rank), jnp.float32)
        for c in blocks:
            normed = (x_at(c) * scale0).astype(BF16)
            n0[:, c] = normed
            low0 = low0 + contract_last(normed, w[0, 0, :, c])
        low0_bf = low0.astype(BF16)
        part = jnp.zeros((rows, 128), jnp.float32)
        for c in blocks:
            hidden = x_at(c) + expand(low0_bf, w[1, 0, :, c])
            h1[:, c] = hidden
            part = part + lane_sum(hidden * hidden)
        scale1 = lax.rsqrt(mean_of(part) + EPSILON)
        low1 = jnp.zeros((rows, rank), jnp.float32)
        for c in blocks:
            normed = (h1[:, c] * scale1).astype(BF16)
            n1[:, c] = normed
            low1 = low1 + contract_last(normed, w[0, 1, :, c])
        back1_bf = back1.astype(BF16)
        mean = jnp.sum(back1_bf.astype(jnp.float32) * low1, axis=-1, keepdims=True) / width
        pull = scale1 * scale1 * mean
        low1_bf = low1.astype(BF16)
        back0 = jnp.zeros((rows, rank), jnp.float32)
        for c in blocks:
            hidden = h1[:, c]
            out = hidden + expand(low1_bf, w[1, 1, :, c])
            out_buf[k, :, c] = out.reshape(GROUP, MB, block).astype(BF16)
            grad = g_at(c) + (scale1 * expand(back1_bf, w[0, 1, :, c]) - hidden * pull)
            grad = grad.astype(BF16)
            g1[:, c] = grad
            back0 = back0 + contract_last(grad, w[1, 0, :, c])

        @pl.loop(i * GROUP, jnp.minimum(n, (i + 1) * GROUP))
        def _(j):
            pltpu.make_async_copy(out_buf.at[j], handed.at[places[j]], out_sem.at[j]).start()

        sides = [
            value.astype(BF16).astype(jnp.float32).T.astype(BF16)
            for value in (back0, back1, low0, low1)
        ]
        for c in blocks:
            terms[0 * rank : 1 * rank, c] += expand(sides[0], n0[:, c])
            terms[1 * rank : 2 * rank, c] += expand(sides[1], n1[:, c])
            terms[2 * rank : 3 * rank, c] += expand(sides[2], g1[:, c])
            terms[3 * rank : 4 * rank, c] += expand(sides[3], g_at(c).astype(BF16))

    if last:
        part_width = width // plan.peers
        for z in range(plan.chips):
            if part_width % 128 == 0:
                start = pl.multiple_of((2 * z + parity) * part_width, 128)
                mine = terms[:, pl.ds(start, part_width)]
                start = pl.multiple_of((2 * z + 1 - parity) * part_width, 128)
                theirs = terms[:, pl.ds(start, part_width)]
            else:
                even = terms[:, 2 * z * part_width : (2 * z + 1) * part_width]
                odd = terms[:, (2 * z + 1) * part_width : (2 * z + 2) * part_width]
                mine = jnp.where(parity == 0, even, odd)
                theirs = jnp.where(parity == 0, odd, even)
            keep[z] = mine
            give[z] = theirs.astype(BF16)
    else:
        copy = pltpu.make_async_copy(terms, terms_out, t_sem)
        copy.start()
        copy.wait()

    @pl.loop(0, n)
    def _(j):
        pltpu.make_async_copy(out_buf.at[j], handed.at[places[j]], out_sem.at[j]).wait()

    if first:

        @pl.loop(total, capacity)
        def _(k):
            pltpu.make_async_copy(out_buf.at[capacity], handed.at[k], zero_sem.at[k]).wait()


def run_step(plan, rank, routes, maps, sources, returned, weights, carried=None, last=False):
    width = returned.shape[-1]
    first = carried is None
    capacity = plan.capacity
    padded = -(-capacity // GROUP) * GROUP
    counts = [len(group) for group in sources]
    flat = [array for group in sources for array in group]
    rows = 4 * rank
    part = (plan.chips, rows, width // plan.peers)
    out_shape = [jax.ShapeDtypeStruct((capacity, MB, width), BF16)]
    out_specs = [HBM]
    if last:
        vmem = pl.BlockSpec(memory_space=pltpu.VMEM)
        out_shape += [jax.ShapeDtypeStruct(part, jnp.float32), jax.ShapeDtypeStruct(part, BF16)]
        out_specs += [vmem, vmem]
    else:
        out_shape += [jax.ShapeDtypeStruct((rows, width), jnp.float32)]
        out_specs += [HBM]
    before = 1 + len(maps) + len(flat) + 3
    return pl.pallas_call(
        functools.partial(step_kernel, plan, rank, counts, first, last),
        out_shape=out_shape,
        in_specs=[SMEM] * (1 + len(maps)) + [HBM] * (len(flat) + 3 + (0 if first else 2)),
        out_specs=out_specs,
        input_output_aliases={} if first else {before: 0},
        scratch_shapes=[
            pltpu.VMEM((padded, MB, width), BF16),
            pltpu.VMEM((padded, MB, width), BF16),
            pltpu.VMEM((padded + 1, MB, width), BF16),
            pltpu.VMEM((GROUP * MB, width), BF16),
            pltpu.VMEM((GROUP * MB, width), BF16),
            pltpu.VMEM((GROUP * MB, width), BF16),
            pltpu.VMEM((GROUP * MB, width), jnp.float32),
            pltpu.VMEM((2, 2, rank, width), BF16),
            pltpu.VMEM((rows, width), jnp.float32),
            pltpu.SemaphoreType.DMA((padded,)),
            pltpu.SemaphoreType.DMA((padded,)),
            pltpu.SemaphoreType.DMA((padded,)),
            pltpu.SemaphoreType.DMA((2,)),
            pltpu.SemaphoreType.DMA,
            pltpu.SemaphoreType.DMA((padded,)),
            pltpu.SMEM((padded,), jnp.int32),
        ],
        compiler_params=pltpu.CompilerParams(vmem_limit_bytes=VMEM_LIMIT),
    )(routes, *maps, *flat, returned, *weights, *(() if first else carried))


def pair_kernel(groups, keep, got, *outs):
    half = lax.div(lax.axis_index("peer"), 2)
    for e in range(groups):
        z = half ^ e
        outs[e][...] = (keep[z] + got[z].astype(jnp.float32)).astype(outs[e].dtype)


def exchange(plan, buffers):
    own = [None] * plan.chips
    for e in reversed(range(plan.chips)):
        own[e] = lax.ppermute(buffers[e], ("section", "peer"), hop_pairs(plan, 1, 2 * e))
    return own


def shards(inbox, routes, adapter_in, adapter_out, returned):
    peers = lax.axis_size("peer")
    sections = lax.axis_size("section")
    tokens, width = inbox.shape[2:]
    layers, rank = adapter_in.shape[1:3]
    micro = tokens // MB
    capacity = returned.shape[2] // MB
    plan = Plan(sections, peers, micro, capacity)
    chips = plan.chips
    axes = ("section", "peer")
    blocks = inbox[0, 0].reshape(micro, MB, width)
    cotangents = returned[0, 0].reshape(capacity, MB, width)

    sent = run_send(plan, plan.sets, routes, blocks, (adapter_in[0], adapter_out[0]))
    own = [exchange(plan, sent[:chips])]
    w_half = lax.ppermute(sent[-1], axes, hop_pairs(plan, 1, 0))
    for i in range(1, len(plan.sets)):
        own.append(exchange(plan, sent[i * chips : (i + 1) * chips]))
    tables = run_tables(plan, routes)
    both = [[*group, *[to_sibling(plan, array) for array in group]] for group in own[:1]]
    weights = (w_half, to_sibling(plan, w_half))
    step = functools.partial(run_step, plan, rank, routes)
    if plan.relay:
        extra_map, picks, relay_map, fits = tables[2:]
        picked = run_picks(plan, picks, both[0])
        relayed = [
            lax.ppermute(array, "peer", [(p, p ^ (2 * f)) for p in range(peers)])
            for f, array in zip(range(1, chips), picked)
        ]
        carried = step([tables[0]], both, cotangents, weights)

        def direct(handed, terms):
            extra = run_send(plan, [(plan.base, plan.full)], routes, blocks)
            group = exchange(plan, extra)
            group = [*group, *[to_sibling(plan, array) for array in group]]
            return tuple(
                step([extra_map], [group], cotangents, weights, carried=(handed, terms))
            )

        carried = lax.cond(fits[0] == 1, lambda *kept: kept, direct, *carried)
        late = [*own[1], *[to_sibling(plan, array) for array in own[1]]]
        relayed = [*relayed, *[to_sibling(plan, array) for array in relayed]]
        handed, keep, give = step(
            [tables[1], relay_map], [late, relayed], cotangents, weights, carried=carried, last=True
        )
    else:
        handed, keep, give = step([tables[0]], both, cotangents, weights, last=True)

    vmem = pl.BlockSpec(memory_space=pltpu.VMEM)
    part_width = width // peers
    got = to_sibling(plan, give)
    summed = pl.pallas_call(
        functools.partial(pair_kernel, chips),
        out_shape=[jax.ShapeDtypeStruct((4 * rank, part_width), BF16)] * chips,
        in_specs=[vmem, vmem],
        out_specs=[vmem] * chips,
        compiler_params=pltpu.CompilerParams(vmem_limit_bytes=VMEM_LIMIT),
    )(keep, got)
    pieces = [
        lax.ppermute(summed[e], axes, hop_pairs(plan, -1, 2 * e)) for e in reversed(range(chips))
    ]
    mean = functools.reduce(jnp.add, [piece.astype(jnp.float32) for piece in pieces]) / peers
    mean = mean.reshape(2, 1, layers, rank, part_width)
    return (handed.reshape(1, 1, capacity * MB, width), mean[0], mean[1])


def solution(mesh):
    return jax.shard_map(
        shards,
        mesh=mesh,
        in_specs=(
            P("section", "peer", None, None),
            P(),
            P("section", None, None, None),
            P("section", None, None, None),
            P("section", "peer", None, None),
        ),
        out_specs=(
            P("section", "peer", None, None),
            P("section", None, None, "peer"),
            P("section", None, None, "peer"),
        ),
        check_vma=False,
    )
```

```python
import functools

import jax
import jax.numpy as jnp
from jax import lax
from jax.experimental import pallas as pl
from jax.experimental.pallas import tpu as pltpu
from jax.sharding import PartitionSpec as P


MB = 8
EPSILON = 1e-06
VMEM_LIMIT = 20 * 2**20
SEND_LIMIT = 8 * 2**20
PREPARE_LIMIT = 12 * 2**20


BF16 = jnp.bfloat16
HBM = pl.BlockSpec(memory_space=pl.ANY)
SMEM = pl.BlockSpec(memory_space=pltpu.SMEM)


class Plan:
    def __init__(self, sections, peers, micro, capacity):
        self.sections, self.peers, self.micro, self.capacity = sections, peers, micro, capacity
        self.chips = peers // 2
        mean = max(1, 2 * micro // peers)
        self.full = 2 * mean
        self.sent = min(self.full, mean + (mean + 1) // 2)
        self.sets = [(0, mean), (mean, self.sent)]
        self.extra = (self.sent, self.full)
        self.spill = min(self.full - self.sent, self.sent - mean)


def hop_pairs(plan, by, offset):
    return [
        (s * plan.peers + p, ((s + by) % plan.sections) * plan.peers + (p ^ offset))
        for s in range(plan.sections)
        for p in range(plan.peers)
    ]


def to_sibling(plan, array):
    return lax.ppermute(array, "peer", [(p, p ^ 1) for p in range(plan.peers)])


def send_kernel(plan, span, weighted, spilling, taking, routes, inbox, *refs):
    chips = plan.chips
    first, end = span
    if weighted:
        weights, refs = refs[:2], refs[2:]
    if taking:
        spilled, refs = refs[0], refs[1:]
    outs, refs = (refs[:chips], refs[chips:]) if end > first else ((), refs)
    if weighted:
        w_out, refs = refs[0], refs[1:]
    if spilling:
        s_out, refs = refs[0], refs[1:]
    stage, sem, out_sem, start, count = refs[:5]
    refs = refs[5:]
    if weighted:
        w_stage, w_sem, refs = refs[0], refs[1], refs[2:]
    if spilling:
        s_stage, s_sem = refs
    section = lax.axis_index("section")
    peer = lax.axis_index("peer")
    chip = lax.div(peer, 2)
    total = jnp.int32(0)
    for c in range(chips):
        load_c = routes[section, peer, 2 * c] + routes[section, peer, 2 * c + 1]
        start[c] = total
        count[c] = load_c
        total = total + load_c

    def pick(e, u):
        return inbox.at[jnp.minimum(start[chip ^ e] + u, plan.micro - 1)]

    def load(e, u):
        return pltpu.make_async_copy(pick(e, u), stage.at[e, u - first], sem.at[e, u - first])

    def store(e):
        return pltpu.make_async_copy(stage.at[e], outs[e], out_sem.at[e])

    if weighted:
        even = lax.rem(peer, 2) == 0
        slots = w_stage.shape[0]
        part = pl.ds(lax.rem(chip, 2) * slots, slots)
        w_load = [pltpu.make_async_copy(weight.at[part], w_stage, w_sem.at[0]) for weight in weights]
        w_store = pltpu.make_async_copy(w_stage, w_out, w_sem.at[1])
        pl.when(even)(lambda: w_load[0].start())
        pl.when(jnp.logical_not(even))(lambda: w_load[1].start())
    order = list(reversed(range(len(outs))))
    for e in order:
        for u in range(first, end):
            if taking and plan.sent - 1 - u < plan.spill:
                own = u < count[chip ^ e]
                other = pltpu.make_async_copy(
                    spilled.at[e, plan.sent - 1 - u], stage.at[e, u - first], sem.at[e, u - first]
                )
                pl.when(own)(lambda: load(e, u).start())
                pl.when(jnp.logical_not(own))(lambda: other.start())
            else:
                load(e, u).start()
    if spilling:
        s_load = [
            pltpu.make_async_copy(pick(e, plan.sent + i), s_stage.at[e, i], s_sem.at[e, i])
            for e in range(chips)
            for i in range(plan.spill)
        ]
        s_store = pltpu.make_async_copy(s_stage, s_out, s_sem.at[chips, 0])
        for copy in s_load:
            copy.start()
    if weighted:
        w_load[0].wait()
        w_store.start()
    for e in order:
        for u in range(first, end):
            load(e, u).wait()
        store(e).start()
    if spilling:
        for copy in s_load:
            copy.wait()
        s_store.start()
    if weighted:
        w_store.wait()
    for e in order:
        store(e).wait()
    if spilling:
        s_store.wait()


def run_send(plan, span, routes, blocks, weights=(), spilling=False, spilled=None):
    width = blocks.shape[-1]
    slots = span[1] - span[0]
    chips = plan.chips if slots else 0
    out_shape = [jax.ShapeDtypeStruct((slots, MB, width), BF16)] * chips
    scratch = [
        pltpu.VMEM((plan.chips, max(1, slots), MB, width), BF16),
        pltpu.SemaphoreType.DMA((plan.chips, max(1, slots))),
        pltpu.SemaphoreType.DMA((plan.chips,)),
        pltpu.SMEM((plan.chips,), jnp.int32),
        pltpu.SMEM((plan.chips,), jnp.int32),
    ]
    if weights:
        quarter = (weights[0].shape[0] // 2, MB, width)
        out_shape.append(jax.ShapeDtypeStruct(quarter, BF16))
        scratch += [pltpu.VMEM(quarter, BF16), pltpu.SemaphoreType.DMA((2,))]
    if spilling:
        spill = (plan.chips, plan.spill, MB, width)
        out_shape.append(jax.ShapeDtypeStruct(spill, BF16))
        scratch += [pltpu.VMEM(spill, BF16), pltpu.SemaphoreType.DMA((plan.chips + 1, plan.spill))]
    taken = () if spilled is None else (spilled,)
    operands = [blocks, *weights, *taken]
    return pl.pallas_call(
        functools.partial(send_kernel, plan, span, bool(weights), spilling, bool(taken)),
        out_shape=out_shape,
        in_specs=[SMEM] + [HBM] * len(operands),
        out_specs=[HBM] * len(out_shape),
        scratch_shapes=scratch,
        compiler_params=pltpu.CompilerParams(vmem_limit_bytes=SEND_LIMIT) if taken else None,
    )(routes, *operands)


def table_kernel(plan, routes, *refs):
    maps, starts = refs[:-1], refs[-1]
    chips = plan.chips
    section = lax.axis_index("section")
    peer = lax.axis_index("peer")
    chip = lax.div(peer, 2)
    core = lax.rem(peer, 2)
    earlier = lax.rem(section + plan.sections - 1, plan.sections)
    total = jnp.int32(0)
    for p in range(plan.peers):
        starts[p] = total
        total = total + routes[earlier, p, peer]
    spans = plan.sets + ([plan.extra] if plan.spill else [])
    fits = jnp.bool_(True)
    if plan.spill:

        def enough(s, fits):
            for z in range(chips):
                for c in range(chips):
                    one, two = (
                        routes[s, 2 * z + lane, 2 * c] + routes[s, 2 * z + lane, 2 * c + 1]
                        for lane in range(2)
                    )
                    over = jnp.maximum(one, two) - plan.sent
                    level = jnp.logical_and(one + two <= 2 * plan.sent, over <= plan.spill)
                    fits = jnp.logical_and(fits, jnp.logical_or(over <= 0, level))
            return fits

        fits = lax.fori_loop(0, plan.sections, enough, fits)
        maps[-1][0] = fits.astype(jnp.int32)

    def place(sender, position, usable):
        zero = routes[earlier, sender, 2 * chip]
        one = routes[earlier, sender, 2 * chip + 1]
        low = jnp.where(core == 1, zero, 0)
        high = jnp.where(core == 1, zero + one, zero)
        mine = jnp.logical_and(position >= low, position < high)
        return jnp.where(jnp.logical_and(mine, usable), starts[sender] + position - low, -1)

    for (a, b), out in zip(spans, maps):
        for lane in range(2):
            for e in range(chips):
                sender = 2 * (chip ^ e) + (core ^ lane)
                load = routes[earlier, sender, 2 * chip] + routes[earlier, sender, 2 * chip + 1]
                for u in range(a, b):
                    slot = place(sender, u, True)
                    item = plan.sent - 1 - u
                    if 0 <= item < plan.spill:
                        usable = jnp.logical_and(fits, u >= load)
                        other = place(sender ^ 1, plan.sent + item, usable)
                        slot = jnp.maximum(slot, other)
                    out[(lane * chips + e) * (b - a) + u - a] = slot


def run_tables(plan, routes):
    spans = plan.sets + ([plan.extra] if plan.spill else [])
    sizes = [2 * plan.chips * (b - a) for a, b in spans] + [1] * bool(plan.spill)
    return pl.pallas_call(
        functools.partial(table_kernel, plan),
        out_shape=[jax.ShapeDtypeStruct((n,), jnp.int32) for n in sizes],
        in_specs=[SMEM],
        out_specs=[SMEM] * len(sizes),
        scratch_shapes=[pltpu.SMEM((plan.peers,), jnp.int32)],
    )(routes)


def contract_last(left, right):
    return lax.dot_general(
        left, right, (((1,), (1,)), ((), ())), preferred_element_type=jnp.float32
    )


def expand(left, right):
    return jnp.dot(left, right, preferred_element_type=jnp.float32)


def column_block(width):
    for block in (1024, 512, 256, 128):
        if width % block == 0:
            return block
    return width


def prepare_kernel(rank, group, returned, *refs):
    quarters, refs = refs[:4], refs[4:]
    rows_out, w, back = refs[:3]
    g_buf, w_buf, sem = refs[3:]
    capacity, _, width = g_buf.shape
    block = column_block(width)
    blocks = [slice(c * block, (c + 1) * block) for c in range(width // block)]
    peer = lax.axis_index("peer")
    parity, half = lax.rem(peer, 2), lax.rem(lax.div(peer, 2), 2)
    copies = [pltpu.make_async_copy(returned, g_buf, sem.at[4])]
    for i, quarter in enumerate(quarters):
        target = w_buf.at[parity ^ (i // 2), half ^ (i % 2)]
        copies.append(pltpu.make_async_copy(quarter, target, sem.at[i]))
    for copy in copies:
        copy.start()
    for copy in copies:
        copy.wait()
    for tensor in range(2):
        for c in blocks:
            value = w_buf[tensor, :, :, :, c].astype(jnp.float32)
            w[tensor, :, :, c] = value.reshape(-1, rank, block).astype(BF16)
    rows = group * MB

    @pl.loop(0, capacity // group)
    def _(i):
        k = pl.ds(i * group, group)
        r = pl.ds(pl.multiple_of(i * rows, rows), rows)
        total = jnp.zeros((rows, rank), jnp.float32)
        for c in blocks:
            g = g_buf[k, :, c].astype(jnp.float32).reshape(rows, block).astype(BF16)
            rows_out[r, c] = g
            total = total + contract_last(g, w[1, 1, :, c])
        back[r, :] = total.astype(BF16)


def run_prepare(rank, group, returned, quarters):
    capacity, _, width = returned.shape
    vmem = pl.BlockSpec(memory_space=pltpu.VMEM)
    layers = quarters[0].shape[0] * 2 * MB // rank
    return pl.pallas_call(
        functools.partial(prepare_kernel, rank, group),
        out_shape=[
            jax.ShapeDtypeStruct((capacity * MB, width), BF16),
            jax.ShapeDtypeStruct((2, layers, rank, width), BF16),
            jax.ShapeDtypeStruct((capacity * MB, rank), BF16),
        ],
        in_specs=[HBM] * 5,
        out_specs=[vmem] * 3,
        scratch_shapes=[
            pltpu.VMEM((capacity, MB, width), BF16),
            pltpu.VMEM((2, 2, *quarters[0].shape), BF16),
            pltpu.SemaphoreType.DMA((5,)),
        ],
        compiler_params=pltpu.CompilerParams(vmem_limit_bytes=PREPARE_LIMIT),
    )(returned, *quarters)


def step_kernel(plan, rank, group, counts, first, *refs):
    tables, refs = refs[: len(counts)], refs[len(counts) :]
    sources, refs = refs[: sum(counts)], refs[sum(counts) :]
    g_rows, w, back1_rows = refs[:3]
    refs = refs[3:] if first else refs[4:]
    handed, keep, give = refs[:3]
    x_buf, out_buf, xb, hb, g1, h1, small, sem, out_sem, held = refs[3:]
    capacity, _, width = x_buf.shape
    block = column_block(width)
    blocks = [slice(c * block, (c + 1) * block) for c in range(width // block)]
    peer = lax.axis_index("peer")
    parity = lax.rem(peer, 2)
    for k in range(capacity):
        held[k] = 0
    i = 0
    for count, table in zip(counts, tables):
        for j in range(count):
            source = sources[i + j]
            for u in range(source.shape[0]):
                k = table[j * source.shape[0] + u]

                @pl.when(k >= 0)
                def _():
                    held[k] = 1
                    pltpu.make_async_copy(source.at[u], x_buf.at[k], sem.at[k]).start()

        i += count

    @pl.loop(0, capacity)
    def _(k):
        @pl.when(held[k] == 0)
        def _():
            x_buf[k] = jnp.zeros((MB, width), BF16)

    rows = group * MB

    def mean_of(part):
        return jnp.sum(part, axis=-1, keepdims=True) / width

    def lane_sum(value):
        part = value[:, :128]
        for c in range(1, value.shape[1] // 128):
            part = part + value[:, c * 128 : (c + 1) * 128]
        return part

    def send_out(k):
        return pltpu.make_async_copy(out_buf.at[k], handed.at[k], out_sem.at[k])

    def each_sent(k, action):
        if first:
            action()
        else:
            pl.when(held[k] == 1)(action)

    def work(i):
        k = pl.ds(i * group, group)
        r = pl.ds(pl.multiple_of(i * rows, rows), rows)

        @pl.loop(i * group, (i + 1) * group)
        def _(j):
            @pl.when(held[j] == 1)
            def _():
                pltpu.make_async_copy(sources[0].at[0], x_buf.at[j], sem.at[j]).wait()

        part = jnp.zeros((rows, 128), jnp.float32)
        for c in blocks:
            x = x_buf[k, :, c].astype(jnp.float32).reshape(rows, block)
            part = part + lane_sum(x * x)
            xb[r, c] = x.astype(BF16)
        low0 = contract_last(xb[r, :], w[0, 0])
        scale0 = lax.rsqrt(mean_of(part) + EPSILON)
        low0 = (low0 * scale0).astype(BF16)
        part = jnp.zeros((rows, 128), jnp.float32)
        for c in blocks:
            hidden = xb[r, c].astype(jnp.float32) + expand(low0, w[1, 0, :, c])
            h1[:, c] = hidden
            part = part + lane_sum(hidden * hidden)
            hb[r, c] = hidden.astype(BF16)
        low1 = contract_last(hb[r, :], w[0, 1])
        scale1 = lax.rsqrt(mean_of(part) + EPSILON)
        low1 = low1 * scale1
        back1 = back1_rows[r, :]
        mean = jnp.sum(back1.astype(jnp.float32) * low1, axis=-1, keepdims=True) / width
        pull = scale1 * scale1 * mean
        low1 = low1.astype(BF16)
        for c in blocks:
            hidden = h1[:, c]
            out = hidden + expand(low1, w[1, 1, :, c])
            out_buf[k, :, c] = out.reshape(group, MB, block).astype(BF16)
            grad = g_rows[r, c].astype(jnp.float32) + (
                scale1 * expand(back1, w[0, 1, :, c]) - hidden * pull
            )
            g1[r, c] = grad.astype(BF16)
        back0 = contract_last(g1[r, :], w[1, 0])

        @pl.loop(i * group, (i + 1) * group)
        def _(j):
            each_sent(j, lambda: send_out(j).start())

        small[0, r, :] = back0.astype(BF16).astype(jnp.float32) * scale0
        small[1, r, :] = back1.astype(jnp.float32) * scale1
        small[2, r, :] = low0.astype(jnp.float32)
        small[3, r, :] = low1.astype(jnp.float32)

    def rest(i):
        r = pl.ds(pl.multiple_of(i * rows, rows), rows)
        for buffer in (xb, hb, g1):
            buffer[r, :] = jnp.zeros((rows, width), BF16)
        small[:, r, :] = jnp.zeros((4, rows, rank), jnp.float32)

    @pl.loop(0, capacity // group)
    def _(i):
        if first:
            work(i)
        else:
            busy = functools.reduce(jnp.maximum, [held[i * group + j] for j in range(group)])
            pl.when(busy == 1)(lambda: work(i))
            pl.when(busy == 0)(lambda: rest(i))

    sides = [small[l].T.astype(BF16) for l in range(4)]
    others = (xb, hb, g1, g_rows)
    part_width = width // plan.peers
    for z in range(plan.chips):
        for l in range(4):
            at = slice(l * rank, (l + 1) * rank)
            both = expand(sides[l], others[l][:, 2 * z * part_width : 2 * (z + 1) * part_width])
            even, odd = both[:, :part_width], both[:, part_width:]
            keep[z, at, :] = jnp.where(parity == 0, even, odd)
            give[z, at, :] = jnp.where(parity == 0, odd, even).astype(BF16)

    @pl.loop(0, capacity)
    def _(k):
        each_sent(k, lambda: send_out(k).wait())


def run_step(plan, rank, group, tables, sources, prepared, handed=None):
    g_rows = prepared[0]
    rows, width = g_rows.shape
    capacity = plan.capacity
    first = handed is None
    part = (plan.chips, 4 * rank, width // plan.peers)
    vmem = pl.BlockSpec(memory_space=pltpu.VMEM)
    counts = [len(arrays) for arrays in sources]
    flat = [array for arrays in sources for array in arrays]
    carried = () if first else (handed,)
    operands = [*tables, *flat, *prepared, *carried]
    return pl.pallas_call(
        functools.partial(step_kernel, plan, rank, group, counts, first),
        out_shape=[
            jax.ShapeDtypeStruct((capacity, MB, width), BF16),
            jax.ShapeDtypeStruct(part, jnp.float32),
            jax.ShapeDtypeStruct(part, BF16),
        ],
        in_specs=[SMEM] * len(tables) + [HBM] * len(flat) + [vmem] * 3 + [HBM] * len(carried),
        out_specs=[HBM, vmem, vmem],
        input_output_aliases={} if first else {len(operands) - 1: 0},
        scratch_shapes=[
            pltpu.VMEM((capacity, MB, width), BF16),
            pltpu.VMEM((capacity, MB, width), BF16),
            pltpu.VMEM((rows, width), BF16),
            pltpu.VMEM((rows, width), BF16),
            pltpu.VMEM((rows, width), BF16),
            pltpu.VMEM((group * MB, width), jnp.float32),
            pltpu.VMEM((4, rows, rank), jnp.float32),
            pltpu.SemaphoreType.DMA((capacity,)),
            pltpu.SemaphoreType.DMA((capacity,)),
            pltpu.SMEM((capacity,), jnp.int32),
        ],
        compiler_params=pltpu.CompilerParams(vmem_limit_bytes=VMEM_LIMIT),
        cost_estimate=pl.CostEstimate(
            flops=22 * rows * width * rank, bytes_accessed=6 * rows * width, transcendentals=0
        ),
    )(*operands)


def pair_kernel(chips, *refs):
    parts, outs = refs[:-chips], refs[-chips:]
    half = lax.div(lax.axis_index("peer"), 2)
    for e in range(chips):
        z = half ^ e
        total = parts[0][z]
        for part in parts[1:]:
            total = total + part[z].astype(jnp.float32)
        outs[e][...] = total.astype(outs[e].dtype)


def exchange(plan, buffers):
    arrived = [None] * plan.chips
    for e in reversed(range(plan.chips)):
        arrived[e] = lax.ppermute(buffers[e], ("section", "peer"), hop_pairs(plan, 1, 2 * e))
    return arrived


def shards(inbox, routes, adapter_in, adapter_out, returned):
    peers = lax.axis_size("peer")
    sections = lax.axis_size("section")
    tokens, width = inbox.shape[2:]
    layers, rank = adapter_in.shape[1:3]
    micro = tokens // MB
    capacity = returned.shape[2] // MB
    plan = Plan(sections, peers, micro, capacity)
    chips = plan.chips
    axes = ("section", "peer")
    blocks = inbox[0, 0].reshape(micro, MB, width)
    cotangents = returned[0, 0].reshape(capacity, MB, width)

    def share(arrays):
        other = []
        for array in arrays:
            other.append(to_sibling(plan, array))
        return [*arrays, *other]

    halves = [
        weight[0].reshape(layers * rank // MB, MB, width) for weight in (adapter_in, adapter_out)
    ]
    spilling = plan.spill > 0
    sent = run_send(plan, (0, 0), routes, blocks, halves, spilling)
    w_own = lax.ppermute(sent[0], axes, hop_pairs(plan, 1, 0))
    spilled = to_sibling(plan, sent[1]) if spilling else None
    sent = run_send(plan, plan.sets[0], routes, blocks)
    early = exchange(plan, sent)
    tables = run_tables(plan, routes)
    sent = run_send(plan, plan.sets[1], routes, blocks, spilled=spilled)
    late = exchange(plan, sent)
    w_near = lax.ppermute(w_own, "peer", [(p, p ^ 2) for p in range(peers)])
    weights = (w_own, w_near, to_sibling(plan, w_own), to_sibling(plan, w_near))
    group = max(1, capacity // 2)
    prepared = run_prepare(rank, group, cotangents, weights)
    small_group = 4 if capacity % 4 == 0 else 1

    def step_more(table, sources, handed):
        return run_step(plan, rank, small_group, [table], [sources], prepared, handed)

    shared = share(early)
    handed, keep, give = run_step(plan, rank, group, tables[:1], [shared], prepared)
    parts = [keep, to_sibling(plan, give)]
    if spilling:

        def direct(handed, keep):
            extra = exchange(plan, run_send(plan, plan.extra, routes, blocks))
            handed, more, gift = step_more(tables[2], share(extra), handed)
            return handed, keep + more + to_sibling(plan, gift).astype(jnp.float32)

        handed, parts[0] = lax.cond(
            tables[3][0] == 1, lambda *kept: kept, direct, handed, parts[0]
        )
    handed, keep, give = step_more(tables[1], share(late), handed)
    parts += [keep, to_sibling(plan, give)]
    part_width = width // peers
    vmem = pl.BlockSpec(memory_space=pltpu.VMEM)
    summed = pl.pallas_call(
        functools.partial(pair_kernel, chips),
        out_shape=[jax.ShapeDtypeStruct((4 * rank, part_width), BF16)] * chips,
        in_specs=[vmem] * len(parts),
        out_specs=[vmem] * chips,
        compiler_params=pltpu.CompilerParams(vmem_limit_bytes=VMEM_LIMIT),
    )(*parts)
    pieces = [
        lax.ppermute(summed[e], axes, hop_pairs(plan, -1, 2 * e)) for e in reversed(range(chips))
    ]
    mean = functools.reduce(jnp.add, [piece.astype(jnp.float32) for piece in pieces]) / peers
    mean = mean.reshape(2, 1, layers, rank, part_width)
    return (handed.reshape(1, 1, capacity * MB, width), mean[0], mean[1])


def solution(mesh):
    return jax.shard_map(
        shards,
        mesh=mesh,
        in_specs=(
            P("section", "peer", None, None),
            P(),
            P("section", None, None, None),
            P("section", None, None, None),
            P("section", "peer", None, None),
        ),
        out_specs=(
            P("section", "peer", None, None),
            P("section", None, None, "peer"),
            P("section", None, None, "peer"),
        ),
        check_vma=False,
    )
```

```python
import functools

import jax
import jax.numpy as jnp
from jax import lax
from jax.experimental import pallas as pl
from jax.experimental.pallas import tpu as pltpu
from jax.sharding import PartitionSpec as P


MB = 8
EPSILON = 1e-06
VMEM_LIMIT = 20 * 2**20
SEND_LIMIT = 8 * 2**20
PREPARE_LIMIT = 12 * 2**20


BF16 = jnp.bfloat16
HBM = pl.BlockSpec(memory_space=pl.ANY)
SMEM = pl.BlockSpec(memory_space=pltpu.SMEM)


class Plan:
    def __init__(self, sections, peers, micro, capacity):
        self.sections, self.peers, self.micro, self.capacity = sections, peers, micro, capacity
        self.chips = peers // 2
        mean = max(1, 2 * micro // peers)
        self.full = 2 * mean
        self.sent = min(self.full, mean + (mean + 1) // 2)
        self.sets = [(0, mean), (mean, self.sent)]
        self.extra = (self.sent, self.full)
        self.spill = min(self.full - self.sent, self.sent - mean)


def hop_pairs(plan, by, offset):
    return [
        (s * plan.peers + p, ((s + by) % plan.sections) * plan.peers + (p ^ offset))
        for s in range(plan.sections)
        for p in range(plan.peers)
    ]


def to_sibling(plan, array):
    return lax.ppermute(array, "peer", [(p, p ^ 1) for p in range(plan.peers)])


def send_kernel(plan, span, weighted, spilling, taking, routes, inbox, *refs):
    chips = plan.chips
    first, end = span
    if weighted:
        weights, refs = refs[:2], refs[2:]
    if taking:
        spilled, refs = refs[0], refs[1:]
    outs, refs = (refs[:chips], refs[chips:]) if end > first else ((), refs)
    if weighted:
        w_out, refs = refs[0], refs[1:]
    if spilling:
        s_out, refs = refs[0], refs[1:]
    stage, sem, out_sem, start, count = refs[:5]
    refs = refs[5:]
    if weighted:
        w_stage, w_sem, refs = refs[0], refs[1], refs[2:]
    if spilling:
        s_stage, s_sem = refs
    section = lax.axis_index("section")
    peer = lax.axis_index("peer")
    chip = lax.div(peer, 2)
    total = jnp.int32(0)
    for c in range(chips):
        load_c = routes[section, peer, 2 * c] + routes[section, peer, 2 * c + 1]
        start[c] = total
        count[c] = load_c
        total = total + load_c

    def pick(e, u):
        return inbox.at[jnp.minimum(start[chip ^ e] + u, plan.micro - 1)]

    def load(e, u):
        return pltpu.make_async_copy(pick(e, u), stage.at[e, u - first], sem.at[e, u - first])

    def store(e):
        return pltpu.make_async_copy(stage.at[e], outs[e], out_sem.at[e])

    if weighted:
        even = lax.rem(peer, 2) == 0
        slots = w_stage.shape[0]
        part = pl.ds(lax.rem(chip, 2) * slots, slots)
        w_load = [pltpu.make_async_copy(weight.at[part], w_stage, w_sem.at[0]) for weight in weights]
        w_store = pltpu.make_async_copy(w_stage, w_out, w_sem.at[1])
        pl.when(even)(lambda: w_load[0].start())
        pl.when(jnp.logical_not(even))(lambda: w_load[1].start())
    order = list(reversed(range(len(outs))))
    for e in order:
        for u in range(first, end):
            if taking and plan.sent - 1 - u < plan.spill:
                own = u < count[chip ^ e]
                other = pltpu.make_async_copy(
                    spilled.at[e, plan.sent - 1 - u], stage.at[e, u - first], sem.at[e, u - first]
                )
                pl.when(own)(lambda: load(e, u).start())
                pl.when(jnp.logical_not(own))(lambda: other.start())
            else:
                load(e, u).start()
    if spilling:
        s_load = [
            pltpu.make_async_copy(pick(e, plan.sent + i), s_stage.at[e, i], s_sem.at[e, i])
            for e in range(chips)
            for i in range(plan.spill)
        ]
        s_store = pltpu.make_async_copy(s_stage, s_out, s_sem.at[chips, 0])
        for copy in s_load:
            copy.start()
    if weighted:
        w_load[0].wait()
        w_store.start()
    for e in order:
        for u in range(first, end):
            load(e, u).wait()
        store(e).start()
    if spilling:
        for copy in s_load:
            copy.wait()
        s_store.start()
    if weighted:
        w_store.wait()
    for e in order:
        store(e).wait()
    if spilling:
        s_store.wait()


def run_send(plan, span, routes, blocks, weights=(), spilling=False, spilled=None):
    width = blocks.shape[-1]
    slots = span[1] - span[0]
    chips = plan.chips if slots else 0
    out_shape = [jax.ShapeDtypeStruct((slots, MB, width), BF16)] * chips
    scratch = [
        pltpu.VMEM((plan.chips, max(1, slots), MB, width), BF16),
        pltpu.SemaphoreType.DMA((plan.chips, max(1, slots))),
        pltpu.SemaphoreType.DMA((plan.chips,)),
        pltpu.SMEM((plan.chips,), jnp.int32),
        pltpu.SMEM((plan.chips,), jnp.int32),
    ]
    if weights:
        quarter = (weights[0].shape[0] // 2, MB, width)
        out_shape.append(jax.ShapeDtypeStruct(quarter, BF16))
        scratch += [pltpu.VMEM(quarter, BF16), pltpu.SemaphoreType.DMA((2,))]
    if spilling:
        spill = (plan.chips, plan.spill, MB, width)
        out_shape.append(jax.ShapeDtypeStruct(spill, BF16))
        scratch += [pltpu.VMEM(spill, BF16), pltpu.SemaphoreType.DMA((plan.chips + 1, plan.spill))]
    taken = () if spilled is None else (spilled,)
    operands = [blocks, *weights, *taken]
    return pl.pallas_call(
        functools.partial(send_kernel, plan, span, bool(weights), spilling, bool(taken)),
        out_shape=out_shape,
        in_specs=[SMEM] + [HBM] * len(operands),
        out_specs=[HBM] * len(out_shape),
        scratch_shapes=scratch,
        compiler_params=pltpu.CompilerParams(vmem_limit_bytes=SEND_LIMIT) if taken else None,
    )(routes, *operands)


def table_kernel(plan, routes, *refs):
    maps, starts = refs[:-1], refs[-1]
    chips = plan.chips
    section = lax.axis_index("section")
    peer = lax.axis_index("peer")
    chip = lax.div(peer, 2)
    core = lax.rem(peer, 2)
    earlier = lax.rem(section + plan.sections - 1, plan.sections)
    total = jnp.int32(0)
    for p in range(plan.peers):
        starts[p] = total
        total = total + routes[earlier, p, peer]
    spans = plan.sets + ([plan.extra] if plan.spill else [])
    fits = jnp.bool_(True)
    if plan.spill:

        def enough(s, fits):
            for z in range(chips):
                for c in range(chips):
                    one, two = (
                        routes[s, 2 * z + lane, 2 * c] + routes[s, 2 * z + lane, 2 * c + 1]
                        for lane in range(2)
                    )
                    over = jnp.maximum(one, two) - plan.sent
                    level = jnp.logical_and(one + two <= 2 * plan.sent, over <= plan.spill)
                    fits = jnp.logical_and(fits, jnp.logical_or(over <= 0, level))
            return fits

        fits = lax.fori_loop(0, plan.sections, enough, fits)
        maps[-1][0] = fits.astype(jnp.int32)

    def place(sender, position, usable):
        zero = routes[earlier, sender, 2 * chip]
        one = routes[earlier, sender, 2 * chip + 1]
        low = jnp.where(core == 1, zero, 0)
        high = jnp.where(core == 1, zero + one, zero)
        mine = jnp.logical_and(position >= low, position < high)
        return jnp.where(jnp.logical_and(mine, usable), starts[sender] + position - low, -1)

    for (a, b), out in zip(spans, maps):
        for lane in range(2):
            for e in range(chips):
                sender = 2 * (chip ^ e) + (core ^ lane)
                load = routes[earlier, sender, 2 * chip] + routes[earlier, sender, 2 * chip + 1]
                for u in range(a, b):
                    slot = place(sender, u, True)
                    item = plan.sent - 1 - u
                    if 0 <= item < plan.spill:
                        usable = jnp.logical_and(fits, u >= load)
                        other = place(sender ^ 1, plan.sent + item, usable)
                        slot = jnp.maximum(slot, other)
                    out[(lane * chips + e) * (b - a) + u - a] = slot


def run_tables(plan, routes):
    spans = plan.sets + ([plan.extra] if plan.spill else [])
    sizes = [2 * plan.chips * (b - a) for a, b in spans] + [1] * bool(plan.spill)
    return pl.pallas_call(
        functools.partial(table_kernel, plan),
        out_shape=[jax.ShapeDtypeStruct((n,), jnp.int32) for n in sizes],
        in_specs=[SMEM],
        out_specs=[SMEM] * len(sizes),
        scratch_shapes=[pltpu.SMEM((plan.peers,), jnp.int32)],
    )(routes)


def contract_last(left, right):
    return lax.dot_general(
        left, right, (((1,), (1,)), ((), ())), preferred_element_type=jnp.float32
    )


def expand(left, right):
    return jnp.dot(left, right, preferred_element_type=jnp.float32)


def column_block(width):
    for block in (1024, 512, 256, 128):
        if width % block == 0:
            return block
    return width


def prepare_kernel(rank, group, returned, *refs):
    quarters, refs = refs[:4], refs[4:]
    rows_out, w, back = refs[:3]
    g_buf, w_buf, sem = refs[3:]
    capacity, _, width = g_buf.shape
    block = column_block(width)
    blocks = [slice(c * block, (c + 1) * block) for c in range(width // block)]
    peer = lax.axis_index("peer")
    parity, half = lax.rem(peer, 2), lax.rem(lax.div(peer, 2), 2)
    copies = [pltpu.make_async_copy(returned, g_buf, sem.at[4])]
    for i, quarter in enumerate(quarters):
        target = w_buf.at[parity ^ (i // 2), half ^ (i % 2)]
        copies.append(pltpu.make_async_copy(quarter, target, sem.at[i]))
    for copy in copies:
        copy.start()
    for copy in copies:
        copy.wait()
    for tensor in range(2):
        for c in blocks:
            value = w_buf[tensor, :, :, :, c].astype(jnp.float32)
            w[tensor, :, :, c] = value.reshape(-1, rank, block).astype(BF16)
    rows = group * MB

    @pl.loop(0, capacity // group)
    def _(i):
        k = pl.ds(i * group, group)
        r = pl.ds(pl.multiple_of(i * rows, rows), rows)
        total = jnp.zeros((rows, rank), jnp.float32)
        for c in blocks:
            g = g_buf[k, :, c].astype(jnp.float32).reshape(rows, block).astype(BF16)
            rows_out[r, c] = g
            total = total + contract_last(g, w[1, 1, :, c])
        back[r, :] = total.astype(BF16)


def run_prepare(rank, group, returned, quarters):
    capacity, _, width = returned.shape
    vmem = pl.BlockSpec(memory_space=pltpu.VMEM)
    layers = quarters[0].shape[0] * 2 * MB // rank
    return pl.pallas_call(
        functools.partial(prepare_kernel, rank, group),
        out_shape=[
            jax.ShapeDtypeStruct((capacity * MB, width), BF16),
            jax.ShapeDtypeStruct((2, layers, rank, width), BF16),
            jax.ShapeDtypeStruct((capacity * MB, rank), BF16),
        ],
        in_specs=[HBM] * 5,
        out_specs=[vmem] * 3,
        scratch_shapes=[
            pltpu.VMEM((capacity, MB, width), BF16),
            pltpu.VMEM((2, 2, *quarters[0].shape), BF16),
            pltpu.SemaphoreType.DMA((5,)),
        ],
        compiler_params=pltpu.CompilerParams(vmem_limit_bytes=PREPARE_LIMIT),
    )(returned, *quarters)


def step_kernel(plan, rank, group, counts, first, *refs):
    tables, refs = refs[: len(counts)], refs[len(counts) :]
    sources, refs = refs[: sum(counts)], refs[sum(counts) :]
    g_source, w, back1_rows = refs[:3]
    refs = refs[3:] if first else refs[4:]
    handed, keep, give = refs[:3]
    x_buf, out_buf, xb, hb, g1, h1, small, g_rows, sem, out_sem, g_sem, held, ready = refs[3:]
    g_copy = pltpu.make_async_copy(g_source, g_rows, g_sem)
    ready[0] = 0
    capacity, _, width = x_buf.shape
    block = column_block(width)
    blocks = [slice(c * block, (c + 1) * block) for c in range(width // block)]
    peer = lax.axis_index("peer")
    parity = lax.rem(peer, 2)
    for k in range(capacity):
        held[k] = 0
    i = 0
    for count, table in zip(counts, tables):
        for j in range(count):
            source = sources[i + j]
            for u in range(source.shape[0]):
                k = table[j * source.shape[0] + u]

                @pl.when(k >= 0)
                def _():
                    held[k] = 1
                    pltpu.make_async_copy(source.at[u], x_buf.at[k], sem.at[k]).start()

        i += count

    @pl.loop(0, capacity)
    def _(k):
        near = k - lax.rem(k, group)
        busy = functools.reduce(jnp.maximum, [held[near + j] for j in range(group)])

        @pl.when(jnp.logical_and(held[k] == 0, jnp.logical_or(busy == 1, first)))
        def _():
            x_buf[k] = jnp.zeros((MB, width), BF16)

    rows = group * MB

    def mean_of(part):
        return jnp.sum(part, axis=-1, keepdims=True) / width

    def lane_sum(value):
        part = value[:, :128]
        for c in range(1, value.shape[1] // 128):
            part = part + value[:, c * 128 : (c + 1) * 128]
        return part

    def send_out(k):
        return pltpu.make_async_copy(out_buf.at[k], handed.at[k], out_sem.at[k])

    def each_sent(k, action):
        if first:
            action()
        else:
            pl.when(held[k] == 1)(action)

    def work(i):
        k = pl.ds(i * group, group)
        r = pl.ds(pl.multiple_of(i * rows, rows), rows)

        @pl.loop(i * group, (i + 1) * group)
        def _(j):
            @pl.when(held[j] == 1)
            def _():
                pltpu.make_async_copy(sources[0].at[0], x_buf.at[j], sem.at[j]).wait()

        part = jnp.zeros((rows, 128), jnp.float32)
        for c in blocks:
            x = x_buf[k, :, c].astype(jnp.float32).reshape(rows, block)
            part = part + lane_sum(x * x)
            xb[r, c] = x.astype(BF16)
        low0 = contract_last(xb[r, :], w[0, 0])
        scale0 = lax.rsqrt(mean_of(part) + EPSILON)
        low0 = (low0 * scale0).astype(BF16)
        part = jnp.zeros((rows, 128), jnp.float32)
        for c in blocks:
            hidden = xb[r, c].astype(jnp.float32) + expand(low0, w[1, 0, :, c])
            h1[:, c] = hidden
            part = part + lane_sum(hidden * hidden)
            hb[r, c] = hidden.astype(BF16)
        low1 = contract_last(hb[r, :], w[0, 1])
        scale1 = lax.rsqrt(mean_of(part) + EPSILON)
        low1 = low1 * scale1
        back1 = back1_rows[r, :]
        mean = jnp.sum(back1.astype(jnp.float32) * low1, axis=-1, keepdims=True) / width
        pull = scale1 * scale1 * mean
        low1 = low1.astype(BF16)
        pl.when(ready[0] == 1)(g_copy.wait)
        ready[0] = 2
        for c in blocks:
            hidden = h1[:, c]
            out = hidden + expand(low1, w[1, 1, :, c])
            out_buf[k, :, c] = out.reshape(group, MB, block).astype(BF16)
            grad = g_rows[r, c].astype(jnp.float32) + (
                scale1 * expand(back1, w[0, 1, :, c]) - hidden * pull
            )
            g1[r, c] = grad.astype(BF16)
        back0 = contract_last(g1[r, :], w[1, 0])

        @pl.loop(i * group, (i + 1) * group)
        def _(j):
            each_sent(j, lambda: send_out(j).start())

        small[0, r, :] = back0.astype(BF16).astype(jnp.float32) * scale0
        small[1, r, :] = back1.astype(jnp.float32) * scale1
        small[2, r, :] = low0.astype(jnp.float32)
        small[3, r, :] = low1.astype(jnp.float32)

    def rest(i):
        r = pl.ds(pl.multiple_of(i * rows, rows), rows)
        for buffer in (xb, hb, g1):
            buffer[r, :] = jnp.zeros((rows, width), BF16)
        small[:, r, :] = jnp.zeros((4, rows, rank), jnp.float32)

    any_held = functools.reduce(jnp.maximum, [held[k] for k in range(capacity)])

    @pl.when(jnp.logical_or(any_held == 1, first))
    def _():
        g_copy.start()
        ready[0] = 1

    @pl.loop(0, capacity // group)
    def _(i):
        if first:
            work(i)
        else:
            busy = functools.reduce(jnp.maximum, [held[i * group + j] for j in range(group)])
            pl.when(busy == 1)(lambda: work(i))
            pl.when(jnp.logical_and(busy == 0, any_held == 1))(lambda: rest(i))

    def gather_terms():
        sides = [small[l].T.astype(BF16) for l in range(4)]
        others = (xb, hb, g1, g_rows)
        part_width = width // plan.peers
        for z in range(plan.chips):
            for l in range(4):
                at = slice(l * rank, (l + 1) * rank)
                both = expand(sides[l], others[l][:, 2 * z * part_width : 2 * (z + 1) * part_width])
                even, odd = both[:, :part_width], both[:, part_width:]
                keep[z, at, :] = jnp.where(parity == 0, even, odd)
                give[z, at, :] = jnp.where(parity == 0, odd, even).astype(BF16)

    if first:
        gather_terms()
    else:
        pl.when(any_held == 1)(gather_terms)

        @pl.when(any_held == 0)
        def _():
            keep[...] = jnp.zeros(keep.shape, keep.dtype)
            give[...] = jnp.zeros(give.shape, give.dtype)

    @pl.loop(0, capacity)
    def _(k):
        each_sent(k, lambda: send_out(k).wait())


def run_step(plan, rank, group, tables, sources, prepared, handed=None):
    g_rows = prepared[0]
    rows, width = g_rows.shape
    capacity = plan.capacity
    first = handed is None
    part = (plan.chips, 4 * rank, width // plan.peers)
    vmem = pl.BlockSpec(memory_space=pltpu.VMEM)
    counts = [len(arrays) for arrays in sources]
    flat = [array for arrays in sources for array in arrays]
    carried = () if first else (handed,)
    operands = [*tables, *flat, *prepared, *carried]
    return pl.pallas_call(
        functools.partial(step_kernel, plan, rank, group, counts, first),
        out_shape=[
            jax.ShapeDtypeStruct((capacity, MB, width), BF16),
            jax.ShapeDtypeStruct(part, jnp.float32),
            jax.ShapeDtypeStruct(part, BF16),
        ],
        in_specs=[SMEM] * len(tables) + [HBM] * len(flat) + [HBM, vmem, vmem] + [HBM] * len(carried),
        out_specs=[HBM, vmem, vmem],
        input_output_aliases={} if first else {len(operands) - 1: 0},
        scratch_shapes=[
            pltpu.VMEM((capacity, MB, width), BF16),
            pltpu.VMEM((capacity, MB, width), BF16),
            pltpu.VMEM((rows, width), BF16),
            pltpu.VMEM((rows, width), BF16),
            pltpu.VMEM((rows, width), BF16),
            pltpu.VMEM((group * MB, width), jnp.float32),
            pltpu.VMEM((4, rows, rank), jnp.float32),
            pltpu.VMEM((rows, width), BF16),
            pltpu.SemaphoreType.DMA((capacity,)),
            pltpu.SemaphoreType.DMA((capacity,)),
            pltpu.SemaphoreType.DMA,
            pltpu.SMEM((capacity,), jnp.int32),
            pltpu.SMEM((1,), jnp.int32),
        ],
        compiler_params=pltpu.CompilerParams(vmem_limit_bytes=VMEM_LIMIT),
        cost_estimate=pl.CostEstimate(
            flops=22 * rows * width * rank, bytes_accessed=6 * rows * width, transcendentals=0
        ),
    )(*operands)


def pair_kernel(chips, *refs):
    parts, outs = refs[:-chips], refs[-chips:]
    half = lax.div(lax.axis_index("peer"), 2)
    for e in range(chips):
        z = half ^ e
        total = parts[0][z]
        for part in parts[1:]:
            total = total + part[z].astype(jnp.float32)
        outs[e][...] = total.astype(outs[e].dtype)


def exchange(plan, buffers):
    arrived = [None] * plan.chips
    for e in reversed(range(plan.chips)):
        arrived[e] = lax.ppermute(buffers[e], ("section", "peer"), hop_pairs(plan, 1, 2 * e))
    return arrived


def shards(inbox, routes, adapter_in, adapter_out, returned):
    peers = lax.axis_size("peer")
    sections = lax.axis_size("section")
    tokens, width = inbox.shape[2:]
    layers, rank = adapter_in.shape[1:3]
    micro = tokens // MB
    capacity = returned.shape[2] // MB
    plan = Plan(sections, peers, micro, capacity)
    chips = plan.chips
    axes = ("section", "peer")
    blocks = inbox[0, 0].reshape(micro, MB, width)
    cotangents = returned[0, 0].reshape(capacity, MB, width)

    def share(arrays):
        other = []
        for array in arrays:
            other.append(to_sibling(plan, array))
        return [*arrays, *other]

    halves = [
        weight[0].reshape(layers * rank // MB, MB, width) for weight in (adapter_in, adapter_out)
    ]
    spilling = plan.spill > 0
    sent = run_send(plan, plan.sets[0], routes, blocks, halves, spilling)
    w_own = lax.ppermute(sent[chips], axes, hop_pairs(plan, 1, 0))
    spilled = to_sibling(plan, sent[-1]) if spilling else None
    early = exchange(plan, sent[:chips])
    tables = run_tables(plan, routes)
    sent = run_send(plan, plan.sets[1], routes, blocks, spilled=spilled)
    late = exchange(plan, sent)
    w_near = lax.ppermute(w_own, "peer", [(p, p ^ 2) for p in range(peers)])
    weights = (w_own, w_near, to_sibling(plan, w_own), to_sibling(plan, w_near))
    group = max(1, capacity // 2)
    prepared = run_prepare(rank, group, cotangents, weights)
    small_group = 4 if capacity % 4 == 0 else 1

    def step_more(table, sources, handed):
        return run_step(plan, rank, small_group, [table], [sources], prepared, handed)

    sources = [share(early), share(late)]
    handed, keep, give = run_step(plan, rank, group, tables[:2], sources, prepared)
    if spilling:

        def direct(handed, keep):
            extra = exchange(plan, run_send(plan, plan.extra, routes, blocks))
            handed, more, gift = step_more(tables[2], share(extra), handed)
            return handed, keep + more + to_sibling(plan, gift).astype(jnp.float32)

        handed, keep = lax.cond(tables[3][0] == 1, lambda *kept: kept, direct, handed, keep)
    parts = [keep, to_sibling(plan, give)]
    part_width = width // peers
    vmem = pl.BlockSpec(memory_space=pltpu.VMEM)
    summed = pl.pallas_call(
        functools.partial(pair_kernel, chips),
        out_shape=[jax.ShapeDtypeStruct((4 * rank, part_width), BF16)] * chips,
        in_specs=[vmem] * len(parts),
        out_specs=[vmem] * chips,
        compiler_params=pltpu.CompilerParams(vmem_limit_bytes=VMEM_LIMIT),
    )(*parts)
    pieces = [
        lax.ppermute(summed[e], axes, hop_pairs(plan, -1, 2 * e)) for e in reversed(range(chips))
    ]
    mean = functools.reduce(jnp.add, [piece.astype(jnp.float32) for piece in pieces]) / peers
    mean = mean.reshape(2, 1, layers, rank, part_width)
    return (handed.reshape(1, 1, capacity * MB, width), mean[0], mean[1])


def solution(mesh):
    return jax.shard_map(
        shards,
        mesh=mesh,
        in_specs=(
            P("section", "peer", None, None),
            P(),
            P("section", None, None, None),
            P("section", None, None, None),
            P("section", "peer", None, None),
        ),
        out_specs=(
            P("section", "peer", None, None),
            P("section", None, None, "peer"),
            P("section", None, None, "peer"),
        ),
        check_vma=False,
    )
```

```python
import functools

import jax
import jax.numpy as jnp
from jax import lax
from jax.experimental import pallas as pl
from jax.experimental.pallas import tpu as pltpu
from jax.sharding import PartitionSpec as P


MB = 8
EPSILON = 1e-06
VMEM_LIMIT = 16 * 2**20
SEND_LIMIT = 8 * 2**20
PREPARE_LIMIT = 12 * 2**20


BF16 = jnp.bfloat16
HBM = pl.BlockSpec(memory_space=pl.ANY)
SMEM = pl.BlockSpec(memory_space=pltpu.SMEM)


class Plan:
    def __init__(self, sections, peers, micro, capacity):
        self.sections, self.peers, self.micro, self.capacity = sections, peers, micro, capacity
        self.chips = peers // 2
        mean = max(1, 2 * micro // peers)
        self.full = 2 * mean
        self.sent = min(self.full, mean + (mean + 1) // 2)
        first = max(1, 3 * mean // 4)
        self.sets = [(0, first), (first, self.sent)]
        self.extra = (self.sent, self.full)
        self.spill = min(self.full - self.sent, self.sent - mean)


def hop_pairs(plan, by, offset):
    return [
        (s * plan.peers + p, ((s + by) % plan.sections) * plan.peers + (p ^ offset))
        for s in range(plan.sections)
        for p in range(plan.peers)
    ]


def to_sibling(plan, array):
    return lax.ppermute(array, "peer", [(p, p ^ 1) for p in range(plan.peers)])


def send_kernel(plan, span, weighted, spilling, taking, routes, inbox, *refs):
    chips = plan.chips
    first, end = span
    if weighted:
        weights, refs = refs[:2], refs[2:]
    if taking:
        spilled, refs = refs[0], refs[1:]
    outs, refs = (refs[:chips], refs[chips:]) if end > first else ((), refs)
    if weighted:
        w_out, refs = refs[0], refs[1:]
    if spilling:
        s_out, refs = refs[0], refs[1:]
    stage, sem, out_sem, start, count = refs[:5]
    refs = refs[5:]
    if weighted:
        w_stage, w_sem, refs = refs[0], refs[1], refs[2:]
    if spilling:
        s_stage, s_sem = refs
    section = lax.axis_index("section")
    peer = lax.axis_index("peer")
    chip = lax.div(peer, 2)
    total = jnp.int32(0)
    for c in range(chips):
        load_c = routes[section, peer, 2 * c] + routes[section, peer, 2 * c + 1]
        start[c] = total
        count[c] = load_c
        total = total + load_c

    def pick(e, u):
        return inbox.at[jnp.minimum(start[chip ^ e] + u, plan.micro - 1)]

    def load(e, u):
        return pltpu.make_async_copy(pick(e, u), stage.at[e, u - first], sem.at[e, u - first])

    def store(e):
        return pltpu.make_async_copy(stage.at[e], outs[e], out_sem.at[e])

    if weighted:
        even = lax.rem(peer, 2) == 0
        slots = w_stage.shape[0]
        part = pl.ds(lax.rem(chip, 2) * slots, slots)
        w_load = [pltpu.make_async_copy(weight.at[part], w_stage, w_sem.at[0]) for weight in weights]
        w_store = pltpu.make_async_copy(w_stage, w_out, w_sem.at[1])
        pl.when(even)(lambda: w_load[0].start())
        pl.when(jnp.logical_not(even))(lambda: w_load[1].start())
    order = list(reversed(range(len(outs))))
    for e in order:
        for u in range(first, end):
            if taking and plan.sent - 1 - u < plan.spill:
                own = u < count[chip ^ e]
                other = pltpu.make_async_copy(
                    spilled.at[e, plan.sent - 1 - u], stage.at[e, u - first], sem.at[e, u - first]
                )
                pl.when(own)(lambda: load(e, u).start())
                pl.when(jnp.logical_not(own))(lambda: other.start())
            else:
                load(e, u).start()
    if spilling:
        s_load = [
            pltpu.make_async_copy(pick(e, plan.sent + i), s_stage.at[e, i], s_sem.at[e, i])
            for e in range(chips)
            for i in range(plan.spill)
        ]
        s_store = pltpu.make_async_copy(s_stage, s_out, s_sem.at[chips, 0])
        for copy in s_load:
            copy.start()
    if weighted:
        w_load[0].wait()
        w_store.start()
    for e in order:
        for u in range(first, end):
            load(e, u).wait()
        store(e).start()
    if spilling:
        for copy in s_load:
            copy.wait()
        s_store.start()
    if weighted:
        w_store.wait()
    for e in order:
        store(e).wait()
    if spilling:
        s_store.wait()


def run_send(plan, span, routes, blocks, weights=(), spilling=False, spilled=None):
    width = blocks.shape[-1]
    slots = span[1] - span[0]
    chips = plan.chips if slots else 0
    out_shape = [jax.ShapeDtypeStruct((slots, MB, width), BF16)] * chips
    scratch = [
        pltpu.VMEM((plan.chips, max(1, slots), MB, width), BF16),
        pltpu.SemaphoreType.DMA((plan.chips, max(1, slots))),
        pltpu.SemaphoreType.DMA((plan.chips,)),
        pltpu.SMEM((plan.chips,), jnp.int32),
        pltpu.SMEM((plan.chips,), jnp.int32),
    ]
    if weights:
        quarter = (weights[0].shape[0] // 2, MB, width)
        out_shape.append(jax.ShapeDtypeStruct(quarter, BF16))
        scratch += [pltpu.VMEM(quarter, BF16), pltpu.SemaphoreType.DMA((2,))]
    if spilling:
        spill = (plan.chips, plan.spill, MB, width)
        out_shape.append(jax.ShapeDtypeStruct(spill, BF16))
        scratch += [pltpu.VMEM(spill, BF16), pltpu.SemaphoreType.DMA((plan.chips + 1, plan.spill))]
    taken = () if spilled is None else (spilled,)
    operands = [blocks, *weights, *taken]
    return pl.pallas_call(
        functools.partial(send_kernel, plan, span, bool(weights), spilling, bool(taken)),
        out_shape=out_shape,
        in_specs=[SMEM] + [HBM] * len(operands),
        out_specs=[HBM] * len(out_shape),
        scratch_shapes=scratch,
        compiler_params=pltpu.CompilerParams(vmem_limit_bytes=SEND_LIMIT) if taken else None,
    )(routes, *operands)


def table_kernel(plan, routes, *refs):
    maps, starts = refs[:-1], refs[-1]
    chips = plan.chips
    section = lax.axis_index("section")
    peer = lax.axis_index("peer")
    chip = lax.div(peer, 2)
    core = lax.rem(peer, 2)
    earlier = lax.rem(section + plan.sections - 1, plan.sections)
    total = jnp.int32(0)
    for p in range(plan.peers):
        starts[p] = total
        total = total + routes[earlier, p, peer]
    spans = plan.sets + ([plan.extra] if plan.spill else [])
    fits = jnp.bool_(True)
    if plan.spill:

        def enough(s, fits):
            for z in range(chips):
                for c in range(chips):
                    one, two = (
                        routes[s, 2 * z + lane, 2 * c] + routes[s, 2 * z + lane, 2 * c + 1]
                        for lane in range(2)
                    )
                    over = jnp.maximum(one, two) - plan.sent
                    level = jnp.logical_and(one + two <= 2 * plan.sent, over <= plan.spill)
                    fits = jnp.logical_and(fits, jnp.logical_or(over <= 0, level))
            return fits

        fits = lax.fori_loop(0, plan.sections, enough, fits)
        maps[-1][0] = fits.astype(jnp.int32)

    def place(sender, position, usable):
        zero = routes[earlier, sender, 2 * chip]
        one = routes[earlier, sender, 2 * chip + 1]
        low = jnp.where(core == 1, zero, 0)
        high = jnp.where(core == 1, zero + one, zero)
        mine = jnp.logical_and(position >= low, position < high)
        return jnp.where(jnp.logical_and(mine, usable), starts[sender] + position - low, -1)

    for (a, b), out in zip(spans, maps):
        for lane in range(2):
            for e in range(chips):
                sender = 2 * (chip ^ e) + (core ^ lane)
                load = routes[earlier, sender, 2 * chip] + routes[earlier, sender, 2 * chip + 1]
                for u in range(a, b):
                    slot = place(sender, u, True)
                    item = plan.sent - 1 - u
                    if 0 <= item < plan.spill:
                        usable = jnp.logical_and(fits, u >= load)
                        other = place(sender ^ 1, plan.sent + item, usable)
                        slot = jnp.maximum(slot, other)
                    out[(lane * chips + e) * (b - a) + u - a] = slot


def run_tables(plan, routes):
    spans = plan.sets + ([plan.extra] if plan.spill else [])
    sizes = [2 * plan.chips * (b - a) for a, b in spans] + [1] * bool(plan.spill)
    return pl.pallas_call(
        functools.partial(table_kernel, plan),
        out_shape=[jax.ShapeDtypeStruct((n,), jnp.int32) for n in sizes],
        in_specs=[SMEM],
        out_specs=[SMEM] * len(sizes),
        scratch_shapes=[pltpu.SMEM((plan.peers,), jnp.int32)],
    )(routes)


def contract_last(left, right):
    return lax.dot_general(
        left, right, (((1,), (1,)), ((), ())), preferred_element_type=jnp.float32
    )


def expand(left, right):
    return jnp.dot(left, right, preferred_element_type=jnp.float32)


def column_block(width):
    for block in (1024, 512, 256, 128):
        if width % block == 0:
            return block
    return width


def prepare_kernel(rank, group, returned, *refs):
    quarters, refs = refs[:4], refs[4:]
    rows_out, w, back = refs[:3]
    g_buf, w_buf, sem = refs[3:]
    capacity, _, width = g_buf.shape
    block = column_block(width)
    blocks = [slice(c * block, (c + 1) * block) for c in range(width // block)]
    peer = lax.axis_index("peer")
    parity, half = lax.rem(peer, 2), lax.rem(lax.div(peer, 2), 2)
    copies = [pltpu.make_async_copy(returned, g_buf, sem.at[4])]
    for i, quarter in enumerate(quarters):
        target = w_buf.at[parity ^ (i // 2), half ^ (i % 2)]
        copies.append(pltpu.make_async_copy(quarter, target, sem.at[i]))
    for copy in copies:
        copy.start()
    for copy in copies:
        copy.wait()
    for tensor in range(2):
        for c in blocks:
            value = w_buf[tensor, :, :, :, c].astype(jnp.float32)
            w[tensor, :, :, c] = value.reshape(-1, rank, block).astype(BF16)
    rows = group * MB

    @pl.loop(0, capacity // group)
    def _(i):
        k = pl.ds(i * group, group)
        r = pl.ds(pl.multiple_of(i * rows, rows), rows)
        total = jnp.zeros((rows, rank), jnp.float32)
        for c in blocks:
            g = g_buf[k, :, c].astype(jnp.float32).reshape(rows, block).astype(BF16)
            rows_out[r, c] = g
            total = total + contract_last(g, w[1, 1, :, c])
        back[r, :] = total.astype(BF16)


def run_prepare(rank, group, returned, quarters):
    capacity, _, width = returned.shape
    vmem = pl.BlockSpec(memory_space=pltpu.VMEM)
    layers = quarters[0].shape[0] * 2 * MB // rank
    return pl.pallas_call(
        functools.partial(prepare_kernel, rank, group),
        out_shape=[
            jax.ShapeDtypeStruct((capacity * MB, width), BF16),
            jax.ShapeDtypeStruct((2, layers, rank, width), BF16),
            jax.ShapeDtypeStruct((capacity * MB, rank), BF16),
        ],
        in_specs=[HBM] * 5,
        out_specs=[vmem] * 3,
        scratch_shapes=[
            pltpu.VMEM((capacity, MB, width), BF16),
            pltpu.VMEM((2, 2, *quarters[0].shape), BF16),
            pltpu.SemaphoreType.DMA((5,)),
        ],
        compiler_params=pltpu.CompilerParams(vmem_limit_bytes=PREPARE_LIMIT),
    )(returned, *quarters)


def step_kernel(plan, rank, group, counts, first, *refs):
    tables, refs = refs[: len(counts)], refs[len(counts) :]
    sources, refs = refs[: sum(counts)], refs[sum(counts) :]
    g_source, w, back1_rows = refs[:3]
    refs = refs[3:] if first else refs[4:]
    handed, keep, give = refs[:3]
    x_buf, out_buf, xb, hb, g1, h1, small, g_rows, sem, out_sem, g_sem, held, ready = refs[3:]
    g_copy = pltpu.make_async_copy(g_source, g_rows, g_sem)
    ready[0] = 0
    capacity, _, width = x_buf.shape
    block = column_block(width)
    blocks = [slice(c * block, (c + 1) * block) for c in range(width // block)]
    peer = lax.axis_index("peer")
    parity = lax.rem(peer, 2)
    for k in range(capacity):
        held[k] = 0
    i = 0
    for count, table in zip(counts, tables):
        for j in range(count):
            source = sources[i + j]
            for u in range(source.shape[0]):
                k = table[j * source.shape[0] + u]

                @pl.when(k >= 0)
                def _():
                    held[k] = 1
                    pltpu.make_async_copy(source.at[u], x_buf.at[k], sem.at[k]).start()

        i += count

    @pl.loop(0, capacity)
    def _(k):
        near = k - lax.rem(k, group)
        busy = functools.reduce(jnp.maximum, [held[near + j] for j in range(group)])

        @pl.when(jnp.logical_and(held[k] == 0, jnp.logical_or(busy == 1, first)))
        def _():
            x_buf[k] = jnp.zeros((MB, width), BF16)

    rows = group * MB

    def mean_of(part):
        return jnp.sum(part, axis=-1, keepdims=True) / width

    def lane_sum(value):
        part = value[:, :128]
        for c in range(1, value.shape[1] // 128):
            part = part + value[:, c * 128 : (c + 1) * 128]
        return part

    def send_out(k):
        return pltpu.make_async_copy(out_buf.at[k], handed.at[k], out_sem.at[k])

    def each_sent(k, action):
        if first:
            action()
        else:
            pl.when(held[k] == 1)(action)

    def work(i):
        k = pl.ds(i * group, group)
        r = pl.ds(pl.multiple_of(i * rows, rows), rows)

        @pl.loop(i * group, (i + 1) * group)
        def _(j):
            @pl.when(held[j] == 1)
            def _():
                pltpu.make_async_copy(sources[0].at[0], x_buf.at[j], sem.at[j]).wait()

        part = jnp.zeros((rows, 128), jnp.float32)
        for c in blocks:
            x = x_buf[k, :, c].astype(jnp.float32).reshape(rows, block)
            part = part + lane_sum(x * x)
            xb[r, c] = x.astype(BF16)
        low0 = contract_last(xb[r, :], w[0, 0])
        scale0 = lax.rsqrt(mean_of(part) + EPSILON)
        low0 = (low0 * scale0).astype(BF16)
        part = jnp.zeros((rows, 128), jnp.float32)
        for c in blocks:
            hidden = xb[r, c].astype(jnp.float32) + expand(low0, w[1, 0, :, c])
            h1[:, c] = hidden
            part = part + lane_sum(hidden * hidden)
            hb[r, c] = hidden.astype(BF16)
        low1 = contract_last(hb[r, :], w[0, 1])
        scale1 = lax.rsqrt(mean_of(part) + EPSILON)
        low1 = low1 * scale1
        back1 = back1_rows[r, :]
        mean = jnp.sum(back1.astype(jnp.float32) * low1, axis=-1, keepdims=True) / width
        pull = scale1 * scale1 * mean
        low1 = low1.astype(BF16)
        pl.when(ready[0] == 1)(g_copy.wait)
        ready[0] = 2
        for c in blocks:
            hidden = h1[:, c]
            out = hidden + expand(low1, w[1, 1, :, c])
            out_buf[k, :, c] = out.reshape(group, MB, block).astype(BF16)
            grad = g_rows[r, c].astype(jnp.float32) + (
                scale1 * expand(back1, w[0, 1, :, c]) - hidden * pull
            )
            g1[r, c] = grad.astype(BF16)
        back0 = contract_last(g1[r, :], w[1, 0])

        @pl.loop(i * group, (i + 1) * group)
        def _(j):
            each_sent(j, lambda: send_out(j).start())

        small[0, r, :] = back0.astype(BF16).astype(jnp.float32) * scale0
        small[1, r, :] = back1.astype(jnp.float32) * scale1
        small[2, r, :] = low0.astype(jnp.float32)
        small[3, r, :] = low1.astype(jnp.float32)

    def rest(i):
        r = pl.ds(pl.multiple_of(i * rows, rows), rows)
        for buffer in (xb, hb, g1):
            buffer[r, :] = jnp.zeros((rows, width), BF16)
        small[:, r, :] = jnp.zeros((4, rows, rank), jnp.float32)

    any_held = functools.reduce(jnp.maximum, [held[k] for k in range(capacity)])

    @pl.when(jnp.logical_or(any_held == 1, first))
    def _():
        g_copy.start()
        ready[0] = 1

    @pl.loop(0, capacity // group)
    def _(i):
        if first:
            work(i)
        else:
            busy = functools.reduce(jnp.maximum, [held[i * group + j] for j in range(group)])
            pl.when(busy == 1)(lambda: work(i))
            pl.when(jnp.logical_and(busy == 0, any_held == 1))(lambda: rest(i))

    def gather_terms():
        sides = [small[l].T.astype(BF16) for l in range(4)]
        others = (xb, hb, g1, g_rows)
        part_width = width // plan.peers
        for z in range(plan.chips):
            for l in range(4):
                at = slice(l * rank, (l + 1) * rank)
                both = expand(sides[l], others[l][:, 2 * z * part_width : 2 * (z + 1) * part_width])
                even, odd = both[:, :part_width], both[:, part_width:]
                keep[z, at, :] = jnp.where(parity == 0, even, odd)
                give[z, at, :] = jnp.where(parity == 0, odd, even).astype(BF16)

    if first:
        gather_terms()
    else:
        pl.when(any_held == 1)(gather_terms)

        @pl.when(any_held == 0)
        def _():
            keep[...] = jnp.zeros(keep.shape, keep.dtype)
            give[...] = jnp.zeros(give.shape, give.dtype)

    @pl.loop(0, capacity)
    def _(k):
        each_sent(k, lambda: send_out(k).wait())


def run_step(plan, rank, group, tables, sources, prepared, handed=None):
    g_rows = prepared[0]
    rows, width = g_rows.shape
    capacity = plan.capacity
    first = handed is None
    part = (plan.chips, 4 * rank, width // plan.peers)
    vmem = pl.BlockSpec(memory_space=pltpu.VMEM)
    counts = [len(arrays) for arrays in sources]
    flat = [array for arrays in sources for array in arrays]
    carried = () if first else (handed,)
    operands = [*tables, *flat, *prepared, *carried]
    return pl.pallas_call(
        functools.partial(step_kernel, plan, rank, group, counts, first),
        out_shape=[
            jax.ShapeDtypeStruct((capacity, MB, width), BF16),
            jax.ShapeDtypeStruct(part, jnp.float32),
            jax.ShapeDtypeStruct(part, BF16),
        ],
        in_specs=[SMEM] * len(tables) + [HBM] * len(flat) + [HBM, vmem, vmem] + [HBM] * len(carried),
        out_specs=[HBM, vmem, vmem],
        input_output_aliases={} if first else {len(operands) - 1: 0},
        scratch_shapes=[
            pltpu.VMEM((capacity, MB, width), BF16),
            pltpu.VMEM((capacity, MB, width), BF16),
            pltpu.VMEM((rows, width), BF16),
            pltpu.VMEM((rows, width), BF16),
            pltpu.VMEM((rows, width), BF16),
            pltpu.VMEM((group * MB, width), jnp.float32),
            pltpu.VMEM((4, rows, rank), jnp.float32),
            pltpu.VMEM((rows, width), BF16),
            pltpu.SemaphoreType.DMA((capacity,)),
            pltpu.SemaphoreType.DMA((capacity,)),
            pltpu.SemaphoreType.DMA,
            pltpu.SMEM((capacity,), jnp.int32),
            pltpu.SMEM((1,), jnp.int32),
        ],
        compiler_params=pltpu.CompilerParams(vmem_limit_bytes=VMEM_LIMIT),
        cost_estimate=pl.CostEstimate(
            flops=22 * rows * width * rank, bytes_accessed=6 * rows * width, transcendentals=0
        ),
    )(*operands)


def pair_kernel(chips, *refs):
    parts, outs = refs[:-chips], refs[-chips:]
    half = lax.div(lax.axis_index("peer"), 2)
    for e in range(chips):
        z = half ^ e
        total = parts[0][z]
        for part in parts[1:]:
            total = total + part[z].astype(jnp.float32)
        outs[e][...] = total.astype(outs[e].dtype)


def exchange(plan, buffers):
    arrived = [None] * plan.chips
    for e in reversed(range(plan.chips)):
        arrived[e] = lax.ppermute(buffers[e], ("section", "peer"), hop_pairs(plan, 1, 2 * e))
    return arrived


def shards(inbox, routes, adapter_in, adapter_out, returned):
    peers = lax.axis_size("peer")
    sections = lax.axis_size("section")
    tokens, width = inbox.shape[2:]
    layers, rank = adapter_in.shape[1:3]
    micro = tokens // MB
    capacity = returned.shape[2] // MB
    plan = Plan(sections, peers, micro, capacity)
    chips = plan.chips
    axes = ("section", "peer")
    blocks = inbox[0, 0].reshape(micro, MB, width)
    cotangents = returned[0, 0].reshape(capacity, MB, width)

    def share(arrays):
        other = []
        for array in arrays:
            other.append(to_sibling(plan, array))
        return [*arrays, *other]

    halves = [
        weight[0].reshape(layers * rank // MB, MB, width) for weight in (adapter_in, adapter_out)
    ]
    spilling = plan.spill > 0
    sent = run_send(plan, plan.sets[0], routes, blocks, halves)
    w_own = lax.ppermute(sent[chips], axes, hop_pairs(plan, 1, 0))
    early = exchange(plan, sent[:chips])
    spilled = None
    if spilling:
        spilled = run_send(plan, (0, 0), routes, blocks, spilling=True)[0]
        spilled = to_sibling(plan, spilled)
    tables = run_tables(plan, routes)
    sent = run_send(plan, plan.sets[1], routes, blocks, spilled=spilled)
    late = exchange(plan, sent)
    w_near = lax.ppermute(w_own, "peer", [(p, p ^ 2) for p in range(peers)])
    weights = (w_own, w_near, to_sibling(plan, w_own), to_sibling(plan, w_near))
    group = max(1, capacity // 2)
    prepared = run_prepare(rank, group, cotangents, weights)
    small_group = 4 if capacity % 4 == 0 else 1

    def step_more(table, sources, handed):
        return run_step(plan, rank, small_group, [table], [sources], prepared, handed)

    sources = [share(early), share(late)]
    handed, keep, give = run_step(plan, rank, group, tables[:2], sources, prepared)
    if spilling:

        def direct(handed, keep):
            extra = exchange(plan, run_send(plan, plan.extra, routes, blocks))
            handed, more, gift = step_more(tables[2], share(extra), handed)
            return handed, keep + more + to_sibling(plan, gift).astype(jnp.float32)

        handed, keep = lax.cond(tables[3][0] == 1, lambda *kept: kept, direct, handed, keep)
    parts = [keep, to_sibling(plan, give)]
    part_width = width // peers
    vmem = pl.BlockSpec(memory_space=pltpu.VMEM)
    summed = pl.pallas_call(
        functools.partial(pair_kernel, chips),
        out_shape=[jax.ShapeDtypeStruct((4 * rank, part_width), BF16)] * chips,
        in_specs=[vmem] * len(parts),
        out_specs=[vmem] * chips,
        compiler_params=pltpu.CompilerParams(vmem_limit_bytes=VMEM_LIMIT),
    )(*parts)
    pieces = [
        lax.ppermute(summed[e], axes, hop_pairs(plan, -1, 2 * e)) for e in reversed(range(chips))
    ]
    mean = functools.reduce(jnp.add, [piece.astype(jnp.float32) for piece in pieces]) / peers
    mean = mean.reshape(2, 1, layers, rank, part_width)
    return (handed.reshape(1, 1, capacity * MB, width), mean[0], mean[1])


def solution(mesh):
    return jax.shard_map(
        shards,
        mesh=mesh,
        in_specs=(
            P("section", "peer", None, None),
            P(),
            P("section", None, None, None),
            P("section", None, None, None),
            P("section", "peer", None, None),
        ),
        out_specs=(
            P("section", "peer", None, None),
            P("section", None, None, "peer"),
            P("section", None, None, "peer"),
        ),
        check_vma=False,
    )
```
